256 devices in a mesh: tm: 16 (over x_hi, z), tensor: 16 (over x_lo, y, core).
Axes of the slice: x: 4 (x_hi: 2, x_lo: 2; x = x_hi * 2 + x_lo), y: 4, z: 8, core: 2. Of those that a mesh axis runs over, the one named last changes fastest.
Arguments:
- features: bfloat16 [2, 2048, 1536], P(None, 'tm'), may hold values from -6 to 6
- lengths: int32 [2], replicated, may hold values from 512 to 2048, as said below
- norm_gains: float32 [2, 1536], replicated, may hold values from 0.1 to 1.9
- qkv_weight: bfloat16 [3, 1536, 1536], P(None, 'tensor'), may hold values from -0.21650635 to 0.21650635
- pos_weight: bfloat16 [1536, 1536], P('tensor'), may hold values from -0.15625 to 0.15625
- pos_biases: float32 [2, 1536], P(None, 'tensor'), may hold values from -3 to 3
- out_weight: bfloat16 [1536, 1536], P('tensor'), may hold values from -0.15625 to 0.15625
- conv_in_weight: bfloat16 [2, 1536, 1536], P(None, 'tensor'), may hold values from -0.15625 to 0.15625
- depth_kernel: float32 [31, 1536], P(None, 'tensor'), may hold values from -1 to 1
- conv_scale: float32 [1536], P('tensor'), may hold values from 0.1 to 1.9
- conv_shift: float32 [1536], P('tensor'), may hold values from -3 to 3
- conv_out_weight: bfloat16 [1536, 1536], P('tensor'), may hold values from -0.15625 to 0.15625
Outputs:
- encoded: bfloat16 [2, 2048, 1536], P(None, ('tm', 'tensor'))
The draws below stay inside these ranges and needn't reach their ends.
Inputs may be any that keep to these rules, and one draw needn't show every extreme that they name: `lengths`: the first window is whole.
All inputs are finite; a program needn't handle non-finite values.
Results may differ from the reference program's by a relative error of at most 0.017.
Values may be sent and summed in bfloat16 or wider, within the bound.
A program may use at most 64 MiB of HBM per device.

```python
import math
import jax
import jax.numpy as jnp
from jax import lax

D = 1536
HEADS = 16
HD = 96
KERNEL = 31
WINDOWS = 2
FRAMES = 2048


def draw_lengths(key, part):
    remaining = jax.random.randint(jax.random.fold_in(key, 7), (WINDOWS - 1,), FRAMES // 4, FRAMES + 1)
    return jnp.concatenate([jnp.full((1,), FRAMES, jnp.int32), remaining.astype(jnp.int32)])


def draw_features(key, part):
    full_shape = (WINDOWS, FRAMES, D)
    values = jnp.clip(jax.random.normal(jax.random.fold_in(key, 11), full_shape, jnp.float32), -6.0, 6.0)
    return values.astype(jnp.bfloat16)


def draw_qkv_weight(key, part):
    full_shape = (3, HEADS * HD, D)
    weight_scale = (D // 2) ** (-0.5)
    values = jnp.clip(jax.random.normal(jax.random.fold_in(key, 19), full_shape, jnp.float32), -6.0, 6.0) * weight_scale
    return values.astype(jnp.bfloat16)


def level_of(own_key, dims, split, least, high):
    def one(position, blocks):
        heights = jax.random.uniform(jax.random.fold_in(jax.random.fold_in(own_key, 6), position), (blocks,), jnp.float32, least / len(split), high / len(split))
        return jnp.repeat(jnp.exp(heights), dims[position] // blocks).reshape((-1,) + (1,) * (len(dims) - position - 1))

    level = one(*split[0])
    for cut in split[1:]:
        level = level * one(*cut)
    return level


def gaussian(own_key, shape, deviation, limit, shards=(), kind=jnp.bfloat16):
    drawn = jax.random.normal(own_key, shape, jnp.float32) * deviation
    if len(shards) > 0:
        drawn = level_of(own_key, shape, shards, -0.22, 0.18) * drawn
    return jnp.clip(drawn, min=-limit, max=limit).astype(kind)


def setup_inputs(seed: int = 0) -> dict:
    splits = jax.random.split(jax.random.key(seed), 13)
    return {
        "features": draw_features(jax.random.fold_in(splits[12], 71), 0),
        "lengths": draw_lengths(jax.random.fold_in(splits[12], 71), 0),
        "norm_gains": jnp.clip(1.0 + 0.18 * jax.random.normal(splits[2], (2, D), jnp.float32), 0.1, 1.9),
        "qkv_weight": draw_qkv_weight(jax.random.fold_in(splits[12], 71), 0),
        "pos_weight": gaussian(splits[4], (HEADS * HD, D), D ** -0.5, 0.15625, ((0, 16),)),
        "pos_biases": gaussian(splits[5], (2, HEADS * HD), 0.5, 3.0, ((1, 16),), jnp.float32),
        "out_weight": gaussian(splits[6], (HEADS * HD, D), (HEADS * HD) ** -0.5, 0.15625, ((0, 16),)),
        "conv_in_weight": gaussian(splits[7], (2, D, D), D ** -0.5, 0.15625, ((1, 16),)),
        "depth_kernel": gaussian(splits[8], (KERNEL, D), KERNEL ** -0.5, 1.0, ((1, 16),), jnp.float32),
        "conv_scale": jnp.clip(1.0 + 0.18 * jax.random.normal(splits[9], (D,), jnp.float32), 0.1, 1.9),
        "conv_shift": gaussian(splits[10], (D,), 0.5, 3.0, ((0, 16),), jnp.float32),
        "conv_out_weight": gaussian(splits[11], (D, D), D ** -0.5, 0.15625, ((0, 16),)),
    }


epsilon = 1e-05

def layer_norm(values, gain):
    values = values.astype(jnp.float32)
    row_mean = lax.optimization_barrier(jnp.mean(values, axis=-1, keepdims=True))
    centred = values - row_mean
    variance = lax.optimization_barrier(jnp.mean(centred * centred, axis=-1, keepdims=True))
    return centred * lax.rsqrt(variance + epsilon) * gain

def sinusoid(offsets, model_width):
    half_width = model_width // 2
    frequency = jnp.exp(jnp.arange(half_width, dtype=jnp.float32) * (-2.0 * math.log(10000.0) / model_width))
    angles = offsets.astype(jnp.float32)[:, None] * frequency[None, :]
    return jnp.concatenate([jnp.sin(angles), jnp.cos(angles)], axis=1)

def diagonal_take(pos_table, row_count, col_count):
    table_width = pos_table.shape[-1]
    leading = pos_table.shape[:-2]
    flattened = pos_table.reshape(leading + (row_count * table_width,))
    flattened = lax.slice_in_dim(flattened, row_count - 1, row_count - 1 + row_count * (table_width - 1), axis=flattened.ndim - 1)
    return flattened.reshape(leading + (row_count, table_width - 1))[..., :col_count]

def rounded_values(values):
    return lax.optimization_barrier(values.astype(jnp.bfloat16)).astype(jnp.float32)

def reference(features, lengths, norm_gains, qkv_weight, pos_weight, pos_biases, out_weight, conv_in_weight, depth_kernel, conv_scale, conv_shift, conv_out_weight):
    windows, frames, model_width = features.shape
    score_scale = 1.0 / math.sqrt(HD)
    normed = layer_norm(features, norm_gains[0]).astype(jnp.bfloat16)
    projections = jnp.einsum('btd,gcd->btgc', normed.astype(jnp.float32), qkv_weight.astype(jnp.float32))
    query_all = projections[:, :, 0]
    content_q = (query_all + pos_biases[0]).astype(jnp.bfloat16)
    position_q = (query_all + pos_biases[1]).astype(jnp.bfloat16)
    key_rows = projections[:, :, 1].astype(jnp.bfloat16)
    value_rows = projections[:, :, 2].astype(jnp.bfloat16)
    offsets = frames - 1 - jnp.arange(2 * frames - 1, dtype=jnp.int32)
    pos_table = sinusoid(offsets, model_width).astype(jnp.bfloat16)
    relative = jnp.dot(pos_table, pos_weight.T, preferred_element_type=jnp.float32).astype(jnp.bfloat16)
    valid_keys = jnp.arange(frames, dtype=jnp.int32)[None, :] < lengths[:, None]

    def split_heads(values):
        return values.reshape(windows, frames, HEADS, HD).transpose(2, 0, 1, 3)
    head_parts = (split_heads(content_q), split_heads(position_q), split_heads(key_rows), split_heads(value_rows), relative.reshape(2 * frames - 1, HEADS, HD).transpose(1, 0, 2))

    def one_head(parts):
        content_score_part, position_part, key_portion, value_portion, relative_part = parts
        content_scores = jnp.einsum('ncr,nur->ncu', content_score_part.astype(jnp.float32), key_portion.astype(jnp.float32))
        full_pos = jnp.einsum('bqe,me->bqm', position_part.astype(jnp.float32), relative_part.astype(jnp.float32))
        scores = (content_scores + diagonal_take(full_pos, frames, frames)) * score_scale
        key_mask = valid_keys[:, None, :]
        scores = jnp.where(key_mask, scores, -1e+30)
        row_max = lax.optimization_barrier(jnp.max(scores, axis=-1, keepdims=True))
        attention_weights = jnp.where(key_mask, jnp.exp(scores - row_max), 0.0)
        totals = lax.optimization_barrier(jnp.sum(attention_weights, axis=-1, keepdims=True))
        summed_rows = jnp.einsum('ywz,yzm->ywm', rounded_values(attention_weights), value_portion.astype(jnp.float32))
        return summed_rows / totals
    per_head = lax.map(one_head, head_parts)
    head_outputs = per_head.transpose(1, 2, 0, 3).reshape(windows, frames, HEADS * HD).astype(jnp.bfloat16)
    attention = jnp.einsum('btc,cd->btd', head_outputs.astype(jnp.float32), out_weight.astype(jnp.float32))
    hidden = (features.astype(jnp.float32) + attention).astype(jnp.bfloat16)
    normed_two = layer_norm(hidden, norm_gains[1]).astype(jnp.bfloat16)
    widened = jnp.einsum('btd,gcd->btgc', normed_two.astype(jnp.float32), conv_in_weight.astype(jnp.float32))
    gated_units = widened[:, :, 0] * jax.nn.sigmoid(widened[:, :, 1])
    frame_valid = jnp.arange(frames, dtype=jnp.int32)[None, :] < lengths[:, None]
    gated_units = jnp.where(frame_valid[:, :, None], gated_units, 0.0).astype(jnp.bfloat16)
    rim = KERNEL // 2
    padded = jnp.pad(gated_units, ((0, 0), (rim, rim), (0, 0))).astype(jnp.float32)
    depth_sum = jnp.zeros((windows, frames, model_width), jnp.float32)
    for tap_index in range(KERNEL):
        depth_sum = depth_sum + padded[:, tap_index:tap_index + frames] * depth_kernel[tap_index]
    affine = depth_sum * conv_scale + conv_shift
    activated = (affine * jax.nn.sigmoid(affine)).astype(jnp.bfloat16)
    conv_part = jnp.einsum('btc,cd->btd', activated.astype(jnp.float32), conv_out_weight.astype(jnp.float32))
    return (hidden.astype(jnp.float32) + conv_part).astype(jnp.bfloat16)
```

```python
import math

import jax
import jax.numpy as jnp
from jax import lax
from jax.experimental import pallas as pl
from jax.experimental.pallas import tpu as pltpu
from jax.sharding import PartitionSpec as P

MESH = pl.DeviceIdType.MESH
HD = 96
D = 1536
HALF = D // 2
TILE = 128
EPS = 1e-05
F32 = jnp.float32
BF16 = jnp.bfloat16


def layer_norm(values, gain):
    row_mean = jnp.mean(values, axis=-1, keepdims=True)
    centred = values - row_mean
    variance = jnp.mean(centred * centred, axis=-1, keepdims=True)
    return centred * lax.rsqrt(variance + EPS) * gain


def dot_nt(a, b):
    return lax.dot_general(a, b, (((1,), (1,)), ((), ())), preferred_element_type=F32)


def dot_nn(a, b):
    return jnp.dot(a, b, preferred_element_type=F32)


def rcopy(src, dst, send_sem, recv_sem, tm, tensor):
    return pltpu.make_async_remote_copy(
        src_ref=src,
        dst_ref=dst,
        send_sem=send_sem,
        recv_sem=recv_sem,
        device_id=(tm, tensor),
        device_id_type=MESH,
    )


def bulk_wait(ref, sem):
    pltpu.make_async_copy(ref, ref, sem).wait()


def kernel(
    lens,
    feat,
    gains,
    wqkv,
    wpos,
    pbias,
    wout,
    wcin,
    dker,
    cscale,
    cshift,
    wcout,
    out,
    xs,
    normed,
    kv,
    q_content,
    q_position,
    fine_sin,
    fine_cos,
    coarse_sin,
    coarse_cos,
    rot,
    scores,
    wo,
    wc,
    hsend,
    hrecv,
    asend,
    arecv,
    nbuf,
    gbuf,
    kv_send,
    ring_recv,
    cross_recv,
    w_send,
    wy_recv,
    wx_recv,
    ws_recv,
    w_local,
    a2a_send,
    a2a_recv,
    n_send,
    n_recv,
    ns_recv,
    halo_send,
    halo_recv,
):
    t = lax.axis_index("tm")
    s = lax.axis_index("tensor")
    z = t % 8
    base = (t // 8) * 8
    other = 8 - base
    z_right = base + (z + 1) % 8
    z_left = base + (z + 7) % 8
    t_cross = (t + 8) % 16
    core = s % 2
    y = (s // 2) % 4
    x_base = (s // 8) * 8
    sibling = s + 1 - 2 * core
    s_cross = (s + 8) % 16
    score_scale = 1.0 / math.sqrt(HD)

    barrier = pltpu.get_barrier_semaphore()
    peers = [(t, (s + k) % 16) for k in range(1, 16)]
    peers += [(t_cross, s_cross), (t_cross, s), (z_right, s), (z_left, s)]
    peers += [((t + 1) % 16, s), ((t + 15) % 16, s)]
    for peer in peers:
        pl.semaphore_signal(barrier, inc=1, device_id=peer, device_id_type=MESH)

    gain_one = gains[0:1, :]
    for w in range(2):

        @pl.loop(0, 8)
        def _(i, w=w):
            rows = feat[w, pl.ds(pl.multiple_of(i * 16, 16), 16), :].astype(F32)
            xs[w, pl.ds(i * 2, 2)] = rows.reshape(2, 8, D)
            normed[pl.ds(pl.multiple_of(w * TILE + i * 16, 16), 16), :] = layer_norm(
                rows, gain_one
            ).astype(BF16)

    kv[t] = dot_nt(wqkv[1:3].reshape(2 * HD, D), normed[...]).astype(BF16)

    pl.semaphore_wait(barrier, len(peers))

    def block(column, offset):
        return (base if column == 0 else other) + (z + offset) % 8

    def part(v, way, d):
        return kv.at[v] if d < 3 else kv.at[v, pl.ds(HD * way, HD)]

    def ring_send(column, d):
        for way in range(2):
            ref = part(block(column, 8 - d if way == 0 else d), way, d)
            rcopy(
                ref,
                ref,
                kv_send,
                ring_recv.at[way, column, d],
                z_right if way == 0 else z_left,
                s,
            ).start()

    def ring_wait(column, d):
        for way in range(2):
            ref = part(block(column, 7 - d if way == 0 else d + 1), way, d)
            rcopy(
                ref,
                ref,
                kv_send,
                ring_recv.at[way, column, d],
                z_right if way == 0 else z_left,
                s,
            ).wait_recv()

    def y_peer(k):
        return x_base + ((y + k) % 4) * 2 + core

    def weights_start(i, own, buf):
        for k in (1, 3, 2):
            rcopy(own, buf.at[s], w_send.at[i], wy_recv.at[i, 4 - k], t, y_peer(k)).start()
        for half, tm in ((0, t), (1, t_cross)):
            rows = pl.ds(48 * half, 48)
            rcopy(
                own.at[rows], buf.at[s, rows], w_send.at[i], wx_recv.at[i, 0], tm, s_cross
            ).start()
        rcopy(own, buf.at[s], w_send.at[i], ws_recv.at[i], t, sibling).start()
        pltpu.make_async_copy(own, buf.at[s], w_local.at[i]).start()

    def weights_y(i, own, buf, k):
        p = y_peer(k)
        rcopy(own, buf.at[p], w_send.at[i], wy_recv.at[i, k], t, y_peer(k)).wait_recv()
        for half, tm in ((0, t), (1, t_cross)):
            ref = buf.at[p, pl.ds(48 * half, 48)]
            rcopy(ref, ref, w_send.at[i], wx_recv.at[i, k], tm, s_cross).start()
        rcopy(buf.at[p], buf.at[p], w_send.at[i], ws_recv.at[i], t, sibling).start()

    def weights_x(i, buf, k):
        p = (y_peer(k) + 8) % 16
        bulk_wait(buf.at[p], wx_recv.at[i, k])
        rcopy(buf.at[p], buf.at[p], w_send.at[i], ws_recv.at[i], t, sibling).start()

    def weights_end(i, own, buf):
        bulk_wait(buf.at[pl.ds(0, 8)], ws_recv.at[i])
        pltpu.make_async_copy(own, buf.at[s], w_local.at[i]).wait()

    ring_send(0, 0)
    rcopy(kv.at[t], kv.at[t], kv_send, cross_recv, t_cross, s).start()
    weights_start(0, wout, wo)

    query = dot_nt(normed[...], wqkv[0])
    q_content[...] = (query + pbias[0:1, :]).astype(BF16)
    q_position[...] = (query + pbias[1:2, :]).astype(BF16)
    frequency = jnp.exp(
        lax.broadcasted_iota(jnp.int32, (1, HALF), 1).astype(F32)
        * (-2.0 * math.log(10000.0) / D)
    )

    n_ids = lax.broadcasted_iota(jnp.int32, (24, 1), 0)
    coarse = ((t - n_ids) * TILE).astype(F32) * frequency
    coarse_sin[...] = jnp.sin(coarse)
    coarse_cos[...] = jnp.cos(coarse)

    @pl.loop(0, 8)
    def _(i):
        ids = 127 - i * 16 - lax.broadcasted_iota(jnp.int32, (16, 1), 0)
        angle = ids.astype(F32) * frequency
        rows = pl.ds(pl.multiple_of(i * 16, 16), 16)
        fine_sin[rows, :] = jnp.sin(angle)
        fine_cos[rows, :] = jnp.cos(angle)

    def rel_tiles(start, stop):
        @pl.loop(start, stop)
        def _(n):
            a_sin = coarse_sin[pl.ds(n, 1), :]
            a_cos = coarse_cos[pl.ds(n, 1), :]
            f_sin = fine_sin[...]
            f_cos = fine_cos[...]
            pe_sin = (a_sin * f_cos + a_cos * f_sin).astype(BF16)
            pe_cos = (a_cos * f_cos - a_sin * f_sin).astype(BF16)
            rel = dot_nt(wpos[:, 0:HALF], pe_sin) + dot_nt(wpos[:, HALF:D], pe_cos)
            part_scores = dot_nn(q_position[...], rel.astype(BF16))
            for w in range(2):
                rot[n, pl.ds(w * TILE, TILE), :] = pltpu.roll(
                    part_scores[w * TILE : (w + 1) * TILE],
                    1,
                    1,
                    stride=1,
                    stride_axis=0,
                )

    row_ids = lax.broadcasted_iota(jnp.int32, (TILE, TILE), 0)
    col_ids = lax.broadcasted_iota(jnp.int32, (TILE, TILE), 1)

    def content(v):
        for w in range(2):
            rows = pl.ds(w * TILE, TILE)
            value = dot_nn(q_content[rows, :], kv[v, 0:HD, pl.ds(w * TILE, TILE)])
            value = value + jnp.where(col_ids <= row_ids, rot[v, rows, :], rot[v + 1, rows, :])
            valid = v * TILE + col_ids < lens[w]
            scores[v, rows, :] = jnp.where(valid, value * score_scale, -1e30)

    def content_pair(column, d):
        content(block(column, 7 - d))
        content(block(column, d + 1))

    ring_wait(0, 0)
    ring_send(0, 1)
    rel_tiles(0, 4)
    rcopy(kv.at[t_cross], kv.at[t_cross], kv_send, cross_recv, t_cross, s).wait_recv()
    ring_send(1, 0)
    rel_tiles(4, 8)
    ring_wait(0, 1)
    ring_send(0, 2)
    rel_tiles(8, 12)
    ring_wait(1, 0)
    ring_send(1, 1)
    weights_y(0, wout, wo, 1)
    weights_y(0, wout, wo, 3)
    rel_tiles(12, 17)
    ring_wait(0, 2)
    ring_send(0, 3)
    content(t)
    content(t_cross)
    content_pair(0, 0)
    weights_x(0, wo, 0)
    ring_wait(1, 1)
    ring_send(1, 2)
    weights_y(0, wout, wo, 2)
    content_pair(1, 0)
    content_pair(0, 1)
    ring_wait(1, 2)
    ring_send(1, 3)
    ring_wait(0, 3)
    content_pair(0, 2)
    content_pair(1, 1)
    content(block(0, 4))
    weights_x(0, wo, 1)
    weights_x(0, wo, 3)
    content_pair(1, 2)
    ring_wait(1, 3)
    content(block(1, 4))
    weights_x(0, wo, 2)
    weights_start(1, wcout, wc)

    peak = jnp.max(scores[...], axis=0)
    peak = jnp.max(peak, axis=-1, keepdims=True)
    gathered = [jnp.zeros((TILE, HD), F32) for _ in range(2)]
    totals = [jnp.zeros((TILE, TILE), F32) for _ in range(2)]
    for v in range(16):
        for w in range(2):
            rows = slice(w * TILE, (w + 1) * TILE)
            weight = jnp.exp(scores[v, rows, :] - peak[rows])
            weight = jnp.where(v * TILE + col_ids < lens[w], weight, 0.0)
            totals[w] = totals[w] + weight
            gathered[w] = gathered[w] + dot_nt(
                weight.astype(BF16), kv[v, HD : 2 * HD, rows]
            )
    heads = [
        (gathered[w] / jnp.sum(totals[w], axis=-1, keepdims=True)).reshape(16, 8, HD)
        for w in range(2)
    ]

    def exchange(i, send, recv, cells):
        send[:, :, 0:HD] = jnp.concatenate(cells, axis=1).astype(BF16)
        for k in range(1, 16):
            p = (s + k) % 16
            rcopy(send.at[p], recv.at[s], a2a_send.at[i], a2a_recv.at[i], t, p).start()
        own = pltpu.make_async_copy(send.at[s], recv.at[s], a2a_recv.at[i])
        own.start()
        bulk_wait(recv, a2a_recv.at[i])

    exchange(0, hsend, hrecv, heads)
    weights_end(0, wout, wo)
    total = dot_nn(hrecv[0, :, 0:HD], wo[0])
    for k in range(1, 16):
        total = total + dot_nn(hrecv[k, :, 0:HD], wo[k])
    own_rows = jnp.concatenate([xs[0, s], xs[1, s]], axis=0)
    hidden = (own_rows + total).astype(BF16).astype(F32)
    nbuf[s] = layer_norm(hidden, gains[1:2, :]).astype(BF16)

    steps = [(1, 0), (0, 1), (0, 3), (1, 1), (1, 3), (0, 2), (1, 2)]

    def n_peer(dx, dy):
        return (x_base + 8 * dx) % 16 + ((y + dy) % 4) * 2 + core

    for j, (dx, dy) in enumerate(steps):
        rcopy(
            nbuf.at[s], nbuf.at[s], n_send, n_recv.at[dx * 4 + (4 - dy) % 4], t, n_peer(dx, dy)
        ).start()
    rcopy(nbuf.at[s], nbuf.at[s], n_send, ns_recv, t, sibling).start()
    for dx, dy in steps:
        p = n_peer(dx, dy)
        rcopy(nbuf.at[p], nbuf.at[p], n_send, n_recv.at[dx * 4 + dy], t, p).wait_recv()
        rcopy(nbuf.at[p], nbuf.at[p], n_send, ns_recv, t, sibling).start()
    bulk_wait(nbuf.at[pl.ds(0, 8)], ns_recv)

    rows_all = nbuf[...].reshape(256, D)
    opened = dot_nt(rows_all, wcin[0])
    gate = dot_nt(rows_all, wcin[1])
    gated = opened * jax.nn.sigmoid(gate)
    ids = lax.broadcasted_iota(jnp.int32, (256, HD), 0)
    window = (ids // 8) % 2
    frame = t * TILE + (ids // 16) * 8 + ids % 8
    limit = jnp.where(window == 0, lens[0], lens[1])
    gated = jnp.where(frame < limit, gated, 0.0).astype(BF16).astype(F32)
    gated = gated.reshape(16, 2, 8, HD)
    for w in range(2):
        gbuf[w, 16:144, 0:HD] = gated[:, w].reshape(TILE, HD)

    def halo(way):
        src = gbuf.at[:, pl.ds(16 if way == 0 else 128, 16), :]
        dst = gbuf.at[:, pl.ds(144 if way == 0 else 0, 16), :]
        tm = (t + 15) % 16 if way == 0 else (t + 1) % 16
        return rcopy(src, dst, halo_send.at[way], halo_recv.at[way], tm, s)

    halo(0).start()
    halo(1).start()
    for k in (1, 3, 2):
        weights_y(1, wcout, wc, k)
    halo(0).wait_recv()
    halo(1).wait_recv()

    @pl.when(t == 0)
    def _():
        gbuf[:, 0:16, :] = jnp.zeros((2, 16, TILE), F32)

    @pl.when(t == 15)
    def _():
        gbuf[:, 144:160, :] = jnp.zeros((2, 16, TILE), F32)

    cells = []
    for w in range(2):
        depth_sum = jnp.zeros((TILE, HD), F32)
        for k in range(31):
            depth_sum = depth_sum + gbuf[w, k + 1 : k + 1 + TILE, 0:HD] * dker[k : k + 1, :]
        affine = depth_sum * cscale[...] + cshift[...]
        cells.append((affine * jax.nn.sigmoid(affine)).reshape(16, 8, HD))

    for k in range(4):
        weights_x(1, wc, k)
    exchange(1, asend, arecv, cells)
    weights_end(1, wcout, wc)
    final = dot_nn(arecv[0, :, 0:HD], wc[0])
    for k in range(1, 16):
        final = final + dot_nn(arecv[k, :, 0:HD], wc[k])
    out[...] = (hidden + final).reshape(2, 8, D).astype(BF16)

    bulk_wait(kv.at[pl.ds(0, 15)], kv_send)
    for i, buf in ((0, wo), (1, wc)):
        bulk_wait(buf.at[pl.ds(0, 15)], w_send.at[i])
    for i, buf in ((0, hsend), (1, asend)):
        bulk_wait(buf.at[pl.ds(0, 15)], a2a_send.at[i])
    bulk_wait(nbuf.at[pl.ds(0, 15)], n_send)
    halo(0).wait_send()
    halo(1).wait_send()


def shards(
    features,
    lengths,
    norm_gains,
    qkv_weight,
    pos_weight,
    pos_biases,
    out_weight,
    conv_in_weight,
    depth_kernel,
    conv_scale,
    conv_shift,
    conv_out_weight,
):
    vmem = pl.BlockSpec(memory_space=pltpu.VMEM)
    dma = pltpu.SemaphoreType.DMA
    return pl.pallas_call(
        kernel,
        out_shape=jax.ShapeDtypeStruct((2, 8, D), BF16),
        in_specs=[pl.BlockSpec(memory_space=pltpu.SMEM)] + [vmem] * 11,
        out_specs=vmem,
        scratch_shapes=[
            pltpu.VMEM((2, 16, 8, D), F32),
            pltpu.VMEM((256, D), BF16),
            pltpu.VMEM((16, 2 * HD, 256), BF16),
            pltpu.VMEM((256, HD), BF16),
            pltpu.VMEM((256, HD), BF16),
            pltpu.VMEM((TILE, HALF), F32),
            pltpu.VMEM((TILE, HALF), F32),
            pltpu.VMEM((24, HALF), F32),
            pltpu.VMEM((24, HALF), F32),
            pltpu.VMEM((17, 256, TILE), F32),
            pltpu.VMEM((16, 256, TILE), F32),
            pltpu.VMEM((16, HD, D), BF16),
            pltpu.VMEM((16, HD, D), BF16),
            pltpu.VMEM((16, 16, TILE), BF16),
            pltpu.VMEM((16, 16, TILE), BF16),
            pltpu.VMEM((16, 16, TILE), BF16),
            pltpu.VMEM((16, 16, TILE), BF16),
            pltpu.VMEM((16, 16, D), BF16),
            pltpu.VMEM((2, 160, TILE), F32),
            dma,
            dma((2, 2, 4)),
            dma,
            dma((2,)),
            dma((2, 4)),
            dma((2, 4)),
            dma((2,)),
            dma((2,)),
            dma((2,)),
            dma((2,)),
            dma,
            dma((8,)),
            dma,
            dma((2,)),
            dma((2,)),
        ],
        compiler_params=pltpu.CompilerParams(
            collective_id=0, has_side_effects=True, vmem_limit_bytes=60 * 2**20
        ),
    )(
        lengths,
        features,
        norm_gains,
        qkv_weight,
        pos_weight,
        pos_biases,
        out_weight,
        conv_in_weight,
        depth_kernel,
        conv_scale.reshape(1, HD),
        conv_shift.reshape(1, HD),
        conv_out_weight,
    )


def solution(mesh):
    return jax.shard_map(
        shards,
        mesh=mesh,
        in_specs=(
            P(None, "tm", None),
            P(),
            P(),
            P(None, "tensor", None),
            P("tensor", None),
            P(None, "tensor"),
            P("tensor", None),
            P(None, "tensor", None),
            P(None, "tensor"),
            P("tensor"),
            P("tensor"),
            P("tensor", None),
        ),
        out_specs=P(None, ("tm", "tensor"), None),
        check_vma=False,
    )
```

```python
import math

import jax
import jax.numpy as jnp
from jax import lax
from jax.experimental import pallas as pl
from jax.experimental.pallas import tpu as pltpu
from jax.sharding import PartitionSpec as P

MESH = pl.DeviceIdType.MESH
HD = 96
D = 1536
HALF = D // 2
TILE = 128
EPS = 1e-05
F32 = jnp.float32
BF16 = jnp.bfloat16


def layer_norm(values, gain):
    row_mean = jnp.mean(values, axis=-1, keepdims=True)
    centred = values - row_mean
    variance = jnp.mean(centred * centred, axis=-1, keepdims=True)
    return centred * lax.rsqrt(variance + EPS) * gain


def dot_nt(a, b):
    return lax.dot_general(a, b, (((1,), (1,)), ((), ())), preferred_element_type=F32)


def dot_nn(a, b):
    return jnp.dot(a, b, preferred_element_type=F32)


def rcopy(src, dst, send_sem, recv_sem, tm, tensor):
    return pltpu.make_async_remote_copy(
        src_ref=src,
        dst_ref=dst,
        send_sem=send_sem,
        recv_sem=recv_sem,
        device_id=(tm, tensor),
        device_id_type=MESH,
    )


def bulk_wait(ref, sem):
    pltpu.make_async_copy(ref, ref, sem).wait()


def kernel(
    lens,
    feat,
    gains,
    wqkv,
    wpos,
    pbias,
    wout,
    wcin,
    dker,
    cscale,
    cshift,
    wcout,
    out,
    xs,
    normed,
    kv,
    q_content,
    q_position,
    fine_sin,
    fine_cos,
    coarse_sin,
    coarse_cos,
    rot,
    scores,
    wbuf,
    params,
    hsend,
    hrecv,
    psend,
    precv,
    pown,
    nbuf,
    gx,
    gbuf,
    kv_send,
    ring_recv,
    cross_recv,
    w_send,
    wx_recv,
    ws_recv,
    w_local,
    a2a_send,
    a2a_recv,
    p_send,
    p_recv,
    n_send,
    n_recv,
    halo_send,
    halo_recv,
    params_send,
    params_recv,
):
    t = lax.axis_index("tm")
    s = lax.axis_index("tensor")
    z = t % 8
    base = (t // 8) * 8
    other = 8 - base
    z_right = base + (z + 1) % 8
    z_left = base + (z + 7) % 8
    t_cross = (t + 8) % 16
    core = s % 2
    y = (s // 2) % 4
    x = s // 8
    g = x * 2 + core
    sibling = s + 1 - 2 * core
    s_cross = (s + 8) % 16
    g_cross = (1 - x) * 2 + core
    t_next = (t + x) % 16
    t_prev = (t + 15 + x) % 16
    edge = [(1 - x) * 8 + y * 2 + cc for cc in range(2)]

    def y_peer(k):
        return x * 8 + ((y + k) % 4) * 2 + core

    def g_peer(k):
        p = (g + k) % 4
        return p, (p // 2) * 8 + y * 2 + p % 2

    score_scale = 1.0 / math.sqrt(HD)

    barrier = pltpu.get_barrier_semaphore()
    peers = [(t, y_peer(k)) for k in range(1, 4)]
    peers += [(t, g_peer(k)[1]) for k in range(1, 4)]
    peers += [(t_cross, s_cross), (t_cross, s), (z_right, s), (z_left, s)]
    peers += [(t_next, p) for p in edge] + [(t_prev, p) for p in edge]
    for peer in peers:
        pl.semaphore_signal(barrier, inc=1, device_id=peer, device_id_type=MESH)

    params[g, 0:31, 0:HD] = dker[...]
    params[g, 31:32, 0:HD] = cscale[...]
    params[g, 32:33, 0:HD] = cshift[...]

    gain_one = gains[0:1, :]
    for w in range(2):

        @pl.loop(0, 8)
        def _(i, w=w):
            rows = feat[w, pl.ds(pl.multiple_of(i * 16, 16), 16), :].astype(F32)
            xs[w, pl.ds(i * 2, 2)] = rows.reshape(2, 8, D)
            normed[pl.ds(pl.multiple_of(w * TILE + i * 16, 16), 16), :] = layer_norm(
                rows, gain_one
            ).astype(BF16)

    kv[t] = dot_nt(wqkv[1:3].reshape(2 * HD, D), normed[...]).astype(BF16)

    pl.semaphore_wait(barrier, len(peers))

    def block(column, offset):
        return (base if column == 0 else other) + (z + offset) % 8

    def part(v, way, d):
        return kv.at[v] if d < 3 else kv.at[v, pl.ds(HD * way, HD)]

    def ring_send(column, d):
        for way in range(2):
            ref = part(block(column, 8 - d if way == 0 else d), way, d)
            rcopy(
                ref,
                ref,
                kv_send,
                ring_recv.at[way, column, d],
                z_right if way == 0 else z_left,
                s,
            ).start()

    def ring_wait(column, d):
        for way in range(2):
            ref = part(block(column, 7 - d if way == 0 else d + 1), way, d)
            rcopy(
                ref,
                ref,
                kv_send,
                ring_recv.at[way, column, d],
                z_right if way == 0 else z_left,
                s,
            ).wait_recv()

    own_weights = [wout, wcin.at[0], wcin.at[1], wcout]

    def weights_start(m):
        own = own_weights[m]
        for half, tm in ((0, t), (1, t_cross)):
            rows = pl.ds(48 * half, 48)
            rcopy(
                own.at[rows], wbuf.at[m, g, rows], w_send, wx_recv.at[m], tm, s_cross
            ).start()
        rcopy(own, wbuf.at[m, g], w_send, ws_recv.at[m], t, sibling).start()
        pltpu.make_async_copy(own, wbuf.at[m, g], w_local.at[m]).start()

    def weights_x(m):
        ref = wbuf.at[m, g_cross]
        bulk_wait(ref, wx_recv.at[m])
        rcopy(ref, ref, w_send, ws_recv.at[m], t, sibling).start()

    def weights_end(m):
        bulk_wait(wbuf.at[m, pl.ds(0, 2)], ws_recv.at[m])
        pltpu.make_async_copy(own_weights[m], wbuf.at[m, g], w_local.at[m]).wait()

    ring_send(0, 0)
    rcopy(kv.at[t], kv.at[t], kv_send, cross_recv, t_cross, s).start()
    for m in range(4):
        weights_start(m)
    for k in range(1, 4):
        rcopy(
            params.at[g], params.at[g], params_send, params_recv, t, g_peer(k)[1]
        ).start()

    query = dot_nt(normed[...], wqkv[0])
    q_content[...] = (query + pbias[0:1, :]).astype(BF16)
    q_position[...] = (query + pbias[1:2, :]).astype(BF16)
    frequency = jnp.exp(
        lax.broadcasted_iota(jnp.int32, (1, HALF), 1).astype(F32)
        * (-2.0 * math.log(10000.0) / D)
    )

    n_ids = lax.broadcasted_iota(jnp.int32, (24, 1), 0)
    coarse = ((t - n_ids) * TILE).astype(F32) * frequency
    coarse_sin[...] = jnp.sin(coarse)
    coarse_cos[...] = jnp.cos(coarse)

    @pl.loop(0, 8)
    def _(i):
        ids = 127 - i * 16 - lax.broadcasted_iota(jnp.int32, (16, 1), 0)
        angle = ids.astype(F32) * frequency
        rows = pl.ds(pl.multiple_of(i * 16, 16), 16)
        fine_sin[rows, :] = jnp.sin(angle)
        fine_cos[rows, :] = jnp.cos(angle)

    def rel_tiles(start, stop):
        @pl.loop(start, stop)
        def _(n):
            a_sin = coarse_sin[pl.ds(n, 1), :]
            a_cos = coarse_cos[pl.ds(n, 1), :]
            f_sin = fine_sin[...]
            f_cos = fine_cos[...]
            pe_sin = (a_sin * f_cos + a_cos * f_sin).astype(BF16)
            pe_cos = (a_cos * f_cos - a_sin * f_sin).astype(BF16)
            rel = dot_nt(wpos[:, 0:HALF], pe_sin) + dot_nt(wpos[:, HALF:D], pe_cos)
            part_scores = dot_nn(q_position[...], rel.astype(BF16))
            for w in range(2):
                rot[n, pl.ds(w * TILE, TILE), :] = pltpu.roll(
                    part_scores[w * TILE : (w + 1) * TILE],
                    1,
                    1,
                    stride=1,
                    stride_axis=0,
                )

    row_ids = lax.broadcasted_iota(jnp.int32, (TILE, TILE), 0)
    col_ids = lax.broadcasted_iota(jnp.int32, (TILE, TILE), 1)

    def content(v):
        for w in range(2):
            rows = pl.ds(w * TILE, TILE)
            value = dot_nn(q_content[rows, :], kv[v, 0:HD, pl.ds(w * TILE, TILE)])
            value = value + jnp.where(col_ids <= row_ids, rot[v, rows, :], rot[v + 1, rows, :])
            valid = v * TILE + col_ids < lens[w]
            scores[v, rows, :] = jnp.where(valid, value * score_scale, -1e30)

    def content_pair(column, d):
        content(block(column, 7 - d))
        content(block(column, d + 1))

    ring_wait(0, 0)
    ring_send(0, 1)
    rel_tiles(0, 4)
    rcopy(kv.at[t_cross], kv.at[t_cross], kv_send, cross_recv, t_cross, s).wait_recv()
    ring_send(1, 0)
    rel_tiles(4, 8)
    ring_wait(0, 1)
    ring_send(0, 2)
    rel_tiles(8, 12)
    ring_wait(1, 0)
    ring_send(1, 1)
    rel_tiles(12, 17)
    ring_wait(0, 2)
    ring_send(0, 3)
    content(t)
    content(t_cross)
    content_pair(0, 0)
    weights_x(0)
    ring_wait(1, 1)
    ring_send(1, 2)
    content_pair(1, 0)
    content_pair(0, 1)
    ring_wait(1, 2)
    ring_send(1, 3)
    ring_wait(0, 3)
    content_pair(0, 2)
    content_pair(1, 1)
    content(block(0, 4))
    weights_x(1)
    content_pair(1, 2)
    ring_wait(1, 3)
    content(block(1, 4))
    weights_x(2)
    weights_x(3)

    peak = jnp.max(scores[...], axis=0)
    peak = jnp.max(peak, axis=-1, keepdims=True)
    gathered = [jnp.zeros((TILE, HD), F32) for _ in range(2)]
    totals = [jnp.zeros((TILE, TILE), F32) for _ in range(2)]
    for v in range(16):
        for w in range(2):
            rows = slice(w * TILE, (w + 1) * TILE)
            weight = jnp.exp(scores[v, rows, :] - peak[rows])
            weight = jnp.where(v * TILE + col_ids < lens[w], weight, 0.0)
            totals[w] = totals[w] + weight
            gathered[w] = gathered[w] + dot_nt(
                weight.astype(BF16), kv[v, HD : 2 * HD, rows]
            )
    heads = [
        (gathered[w] / jnp.sum(totals[w], axis=-1, keepdims=True)).reshape(16, 8, HD)
        for w in range(2)
    ]

    cells = jnp.concatenate(heads, axis=1).astype(BF16)
    for p in range(16):
        hsend[(p // 8) * 2 + p % 2, (p // 2) % 4, :, 0:HD] = cells[p]
    for k in range(1, 4):
        p, dev = g_peer(k)
        rcopy(hsend.at[p], hrecv.at[g], a2a_send, a2a_recv, t, dev).start()
    pltpu.make_async_copy(hsend.at[g], hrecv.at[g], a2a_recv).start()
    bulk_wait(hrecv, a2a_recv)

    def reduce_rows(i, total):
        total = total.reshape(4, 16, D)
        psend[i] = total.astype(BF16)
        for k in (2, 1, 3):
            rcopy(
                psend.at[i, (y + k) % 4], precv.at[i, y], p_send.at[i], p_recv.at[i], t, y_peer(k)
            ).start()
        pown[...] = total
        bulk_wait(precv.at[i, pl.ds(0, 3)], p_recv.at[i])
        result = pown[y]
        for k in range(1, 4):
            result = result + precv[i, (y + k) % 4].astype(F32)
        return result

    weights_end(0)
    total = dot_nn(hrecv[0, :, :, 0:HD].reshape(64, HD), wbuf[0, 0])
    for k in range(1, 4):
        total = total + dot_nn(hrecv[k, :, :, 0:HD].reshape(64, HD), wbuf[0, k])
    own_rows = jnp.concatenate([xs[0, s], xs[1, s]], axis=0)
    hidden = (own_rows + reduce_rows(0, total)).astype(BF16).astype(F32)
    nbuf[y] = layer_norm(hidden, gains[1:2, :]).astype(BF16)

    for k in (2, 1, 3):
        rcopy(nbuf.at[y], nbuf.at[y], n_send, n_recv, t, y_peer(k)).start()
    weights_end(1)
    weights_end(2)
    bulk_wait(nbuf.at[pl.ds(0, 3)], n_recv)

    rows_all = nbuf[...].reshape(64, D)
    opened = dot_nt(rows_all, wbuf[1].reshape(4 * HD, D))
    gate = dot_nt(rows_all, wbuf[2].reshape(4 * HD, D))
    gated = opened * jax.nn.sigmoid(gate)
    ids = lax.broadcasted_iota(jnp.int32, (64, 4 * HD), 0)
    window = (ids // 8) % 2
    frame = t * TILE + x * 64 + (ids // 16) * 16 + core * 8 + ids % 8
    limit = jnp.where(window == 0, lens[0], lens[1])
    gated = jnp.where(frame < limit, gated, 0.0).astype(BF16)
    gx[core, 1:5] = gated.reshape(4, 16, 4 * HD)

    for cc in range(2):
        rcopy(gx.at[core, 4], gx.at[core, 0], halo_send, halo_recv, t_next, edge[cc]).start()
        rcopy(gx.at[core, 1], gx.at[core, 5], halo_send, halo_recv, t_prev, edge[cc]).start()
    inner = gx.at[core, pl.ds(1, 4)]
    rcopy(inner, inner, halo_send, halo_recv, t, sibling).start()
    bulk_wait(params.at[pl.ds(0, 3)], params_recv)
    taps = jnp.concatenate([params[k, :, 0:HD] for k in range(4)], axis=1)
    bulk_wait(gx.at[:, pl.ds(0, 4)], halo_recv)

    first = jnp.logical_and(t == 0, x == 0)
    last = jnp.logical_and(t == 15, x == 1)
    for cc in range(2):
        for j in range(6):
            block_rows = gx[cc, j].astype(F32)
            if j == 0:
                block_rows = jnp.where(first, 0.0, block_rows)
            if j == 5:
                block_rows = jnp.where(last, 0.0, block_rows)
            start = pl.multiple_of((2 * j + cc + 1 - core) * 8, 8)
            for w in range(2):
                gbuf[w, pl.ds(start, 8), :] = block_rows[w * 8 : w * 8 + 8]
    sums = [jnp.zeros((8, 4 * HD), F32) for _ in range(8)]
    for k in range(31):
        tap = taps[k : k + 1, :]
        for j in range(4):
            for w in range(2):
                row = 16 * j + 9 + k
                sums[2 * j + w] = sums[2 * j + w] + gbuf[w, row : row + 8, :] * tap
    affine = jnp.concatenate(sums, axis=0) * taps[31:32, :] + taps[32:33, :]
    activated = (affine * jax.nn.sigmoid(affine)).astype(BF16)

    weights_end(3)
    total = dot_nn(activated, wbuf[3].reshape(4 * HD, D))
    final = reduce_rows(1, total)
    out[...] = (hidden + final).reshape(2, 8, D).astype(BF16)

    bulk_wait(kv.at[pl.ds(0, 15)], kv_send)
    bulk_wait(wbuf.at[pl.ds(0, 3)], w_send)
    bulk_wait(params.at[pl.ds(0, 3)], params_send)
    bulk_wait(hsend.at[pl.ds(0, 3)], a2a_send)
    for i in range(2):
        bulk_wait(psend.at[i, pl.ds(0, 3)], p_send.at[i])
    bulk_wait(nbuf.at[pl.ds(0, 3)], n_send)
    bulk_wait(gx.at[:, pl.ds(0, 4)], halo_send)


def shards(
    features,
    lengths,
    norm_gains,
    qkv_weight,
    pos_weight,
    pos_biases,
    out_weight,
    conv_in_weight,
    depth_kernel,
    conv_scale,
    conv_shift,
    conv_out_weight,
):
    vmem = pl.BlockSpec(memory_space=pltpu.VMEM)
    dma = pltpu.SemaphoreType.DMA
    return pl.pallas_call(
        kernel,
        out_shape=jax.ShapeDtypeStruct((2, 8, D), BF16),
        in_specs=[pl.BlockSpec(memory_space=pltpu.SMEM)] + [vmem] * 11,
        out_specs=vmem,
        scratch_shapes=[
            pltpu.VMEM((2, 16, 8, D), F32),
            pltpu.VMEM((256, D), BF16),
            pltpu.VMEM((16, 2 * HD, 256), BF16),
            pltpu.VMEM((256, HD), BF16),
            pltpu.VMEM((256, HD), BF16),
            pltpu.VMEM((TILE, HALF), F32),
            pltpu.VMEM((TILE, HALF), F32),
            pltpu.VMEM((24, HALF), F32),
            pltpu.VMEM((24, HALF), F32),
            pltpu.VMEM((17, 256, TILE), F32),
            pltpu.VMEM((16, 256, TILE), F32),
            pltpu.VMEM((4, 4, HD, D), BF16),
            pltpu.VMEM((4, 40, TILE), F32),
            pltpu.VMEM((4, 4, 16, TILE), BF16),
            pltpu.VMEM((4, 4, 16, TILE), BF16),
            pltpu.VMEM((2, 4, 16, D), BF16),
            pltpu.VMEM((2, 4, 16, D), BF16),
            pltpu.VMEM((4, 16, D), F32),
            pltpu.VMEM((4, 16, D), BF16),
            pltpu.VMEM((2, 6, 16, 4 * HD), BF16),
            pltpu.VMEM((2, 112, 4 * HD), F32),
            dma,
            dma((2, 2, 4)),
            dma,
            dma,
            dma((4,)),
            dma((4,)),
            dma((4,)),
            dma,
            dma,
            dma((2,)),
            dma((2,)),
            dma,
            dma,
            dma,
            dma,
            dma,
            dma,
        ],
        compiler_params=pltpu.CompilerParams(
            collective_id=0, has_side_effects=True, vmem_limit_bytes=60 * 2**20
        ),
    )(
        lengths,
        features,
        norm_gains,
        qkv_weight,
        pos_weight,
        pos_biases,
        out_weight,
        conv_in_weight,
        depth_kernel,
        conv_scale.reshape(1, HD),
        conv_shift.reshape(1, HD),
        conv_out_weight,
    )


def solution(mesh):
    return jax.shard_map(
        shards,
        mesh=mesh,
        in_specs=(
            P(None, "tm", None),
            P(),
            P(),
            P(None, "tensor", None),
            P("tensor", None),
            P(None, "tensor"),
            P("tensor", None),
            P(None, "tensor", None),
            P(None, "tensor"),
            P("tensor"),
            P("tensor"),
            P("tensor", None),
        ),
        out_specs=P(None, ("tm", "tensor"), None),
        check_vma=False,
    )
```

```python
import math

import jax
import jax.numpy as jnp
from jax import lax
from jax.experimental import pallas as pl
from jax.experimental.pallas import tpu as pltpu
from jax.sharding import PartitionSpec as P

MESH = pl.DeviceIdType.MESH
HD = 96
D = 1536
HALF = D // 2
TILE = 128
EPS = 1e-05
F32 = jnp.float32
BF16 = jnp.bfloat16


def layer_norm(values, gain):
    row_mean = jnp.mean(values, axis=-1, keepdims=True)
    centred = values - row_mean
    variance = jnp.mean(centred * centred, axis=-1, keepdims=True)
    return centred * lax.rsqrt(variance + EPS) * gain


def dot_nt(a, b):
    return lax.dot_general(a, b, (((1,), (1,)), ((), ())), preferred_element_type=F32)


def dot_nn(a, b):
    return jnp.dot(a, b, preferred_element_type=F32)


def rcopy(src, dst, send_sem, recv_sem, tm, tensor):
    return pltpu.make_async_remote_copy(
        src_ref=src,
        dst_ref=dst,
        send_sem=send_sem,
        recv_sem=recv_sem,
        device_id=(tm, tensor),
        device_id_type=MESH,
    )


def bulk_wait(ref, sem):
    pltpu.make_async_copy(ref, ref, sem).wait()


def kernel(
    lens,
    feat,
    gains,
    wqkv,
    wpos_in,
    pbias,
    wout,
    wcin,
    dker,
    cscale,
    cshift,
    wcout,
    out,
    normed,
    kv,
    q_content,
    q_position,
    fine_sin,
    fine_cos,
    coarse_sin,
    coarse_cos,
    rot,
    scores,
    wbuf,
    params,
    hsend,
    hrecv,
    psend,
    precv,
    pown,
    nbuf,
    gx,
    gbuf,
    kv_send,
    ring_recv,
    cross_recv,
    w_send,
    wx_recv,
    ws_recv,
    w_local,
    a2a_send,
    a2a_recv,
    p_send,
    p_recv,
    n_send,
    n_recv,
    halo_send,
    halo_recv,
    params_send,
    params_recv,
    wpos,
    wpos_sem,
):
    t = lax.axis_index("tm")
    s = lax.axis_index("tensor")
    z = t % 8
    base = (t // 8) * 8
    other = 8 - base
    z_right = base + (z + 1) % 8
    z_left = base + (z + 7) % 8
    t_cross = (t + 8) % 16
    core = s % 2
    y = (s // 2) % 4
    x = s // 8
    g = x * 2 + core
    sibling = s + 1 - 2 * core
    s_cross = (s + 8) % 16
    g_cross = (1 - x) * 2 + core
    t_next = (t + x) % 16
    t_prev = (t + 15 + x) % 16
    edge = [(1 - x) * 8 + y * 2 + cc for cc in range(2)]

    def y_peer(k):
        return x * 8 + ((y + k) % 4) * 2 + core

    def g_peer(k):
        p = (g + k) % 4
        return p, (p // 2) * 8 + y * 2 + p % 2

    score_scale = 1.0 / math.sqrt(HD)

    barrier = pltpu.get_barrier_semaphore()
    peers = [(t, y_peer(k)) for k in range(1, 4)]
    peers += [(t, g_peer(k)[1]) for k in range(1, 4)]
    peers += [(t_cross, s_cross), (t_cross, s), (z_right, s), (z_left, s)]
    peers += [(t_next, p) for p in edge] + [(t_prev, p) for p in edge]
    for peer in peers:
        pl.semaphore_signal(barrier, inc=1, device_id=peer, device_id_type=MESH)

    wpos_copy = pltpu.make_async_copy(wpos_in, wpos, wpos_sem)
    wpos_copy.start()

    params[g, 0:31, 0:HD] = dker[...]
    params[g, 31:32, 0:HD] = cscale[...]
    params[g, 32:33, 0:HD] = cshift[...]

    gain_one = gains[0:1, :]
    for w in range(2):

        @pl.loop(0, 8, unroll=2)
        def _(i, w=w):
            rows = feat[w, pl.ds(pl.multiple_of(i * 16, 16), 16), :].astype(F32)
            normed[pl.ds(pl.multiple_of(w * TILE + i * 16, 16), 16), :] = layer_norm(
                rows, gain_one
            ).astype(BF16)

    kv[t] = dot_nt(wqkv[1:3].reshape(2 * HD, D), normed[...]).astype(BF16)

    pl.semaphore_wait(barrier, len(peers))

    def block(column, offset):
        return (base if column == 0 else other) + (z + offset) % 8

    def ring_copy(v, way, column, d, h):
        ref = kv.at[v, pl.ds(HD * h, HD)]
        return rcopy(
            ref,
            ref,
            kv_send,
            ring_recv.at[way, column, d, h],
            z_right if way == 0 else z_left,
            s,
        )

    def ring_send(column, d, h):
        for way in range(2):
            if d < 3 or h == way:
                ring_copy(block(column, 8 - d if way == 0 else d), way, column, d, h).start()

    def ring_wait(column, d, h):
        for way in range(2):
            if d < 3 or h == way:
                v = block(column, 7 - d if way == 0 else d + 1)
                ring_copy(v, way, column, d, h).wait_recv()

    def ring_step(column, d, h):
        ring_wait(column, d, h)
        ring_send(column, d + 1, h)

    def cross_copy(v, h):
        ref = kv.at[v, pl.ds(HD * h, HD)]
        return rcopy(ref, ref, kv_send, cross_recv.at[h], t_cross, s)

    own_weights = [wout, wcin.at[0], wcin.at[1], wcout]

    def weights_start(m):
        own = own_weights[m]
        for half, tm in ((0, t), (1, t_cross)):
            rows = pl.ds(48 * half, 48)
            rcopy(
                own.at[rows], wbuf.at[m, g, rows], w_send, wx_recv.at[m], tm, s_cross
            ).start()
        rcopy(own, wbuf.at[m, g], w_send, ws_recv.at[m], t, sibling).start()
        pltpu.make_async_copy(own, wbuf.at[m, g], w_local.at[m]).start()

    def weights_x(m):
        ref = wbuf.at[m, g_cross]
        bulk_wait(ref, wx_recv.at[m])
        rcopy(ref, ref, w_send, ws_recv.at[m], t, sibling).start()

    def weights_end(m):
        bulk_wait(wbuf.at[m, pl.ds(0, 2)], ws_recv.at[m])
        pltpu.make_async_copy(own_weights[m], wbuf.at[m, g], w_local.at[m]).wait()

    for h in range(2):
        ring_send(0, 0, h)
        cross_copy(t, h).start()
    for m in range(4):
        weights_start(m)
    for k in range(1, 4):
        rcopy(
            params.at[g], params.at[g], params_send, params_recv, t, g_peer(k)[1]
        ).start()

    query = dot_nt(normed[...], wqkv[0])
    q_content[...] = (query + pbias[0:1, :]).astype(BF16)
    q_position[...] = (query + pbias[1:2, :]).astype(BF16)
    wpos_copy.wait()
    frequency = jnp.exp(
        lax.broadcasted_iota(jnp.int32, (1, HALF), 1).astype(F32)
        * (-2.0 * math.log(10000.0) / D)
    )

    n_ids = lax.broadcasted_iota(jnp.int32, (24, 1), 0)
    coarse = ((t - n_ids) * TILE).astype(F32) * frequency
    coarse_sin[...] = jnp.sin(coarse)
    coarse_cos[...] = jnp.cos(coarse)

    @pl.loop(0, 8)
    def _(i):
        ids = 127 - i * 16 - lax.broadcasted_iota(jnp.int32, (16, 1), 0)
        angle = ids.astype(F32) * frequency
        rows = pl.ds(pl.multiple_of(i * 16, 16), 16)
        fine_sin[rows, :] = jnp.sin(angle)
        fine_cos[rows, :] = jnp.cos(angle)

    def rel_tiles(start, stop):
        @pl.loop(start, stop)
        def _(n):
            a_sin = coarse_sin[pl.ds(n, 1), :]
            a_cos = coarse_cos[pl.ds(n, 1), :]
            f_sin = fine_sin[...]
            f_cos = fine_cos[...]
            pe_sin = (a_sin * f_cos + a_cos * f_sin).astype(BF16)
            pe_cos = (a_cos * f_cos - a_sin * f_sin).astype(BF16)
            rel = dot_nt(wpos[:, 0:HALF], pe_sin) + dot_nt(wpos[:, HALF:D], pe_cos)
            part_scores = dot_nn(q_position[...], rel.astype(BF16))
            for w in range(2):
                rot[n, pl.ds(w * TILE, TILE), :] = pltpu.roll(
                    part_scores[w * TILE : (w + 1) * TILE],
                    1,
                    1,
                    stride=1,
                    stride_axis=0,
                )

    row_ids = lax.broadcasted_iota(jnp.int32, (TILE, TILE), 0)
    col_ids = lax.broadcasted_iota(jnp.int32, (TILE, TILE), 1)

    def content(v):
        for w in range(2):
            rows = pl.ds(w * TILE, TILE)
            value = dot_nn(q_content[rows, :], kv[v, 0:HD, pl.ds(w * TILE, TILE)])
            value = value + jnp.where(col_ids <= row_ids, rot[v, rows, :], rot[v + 1, rows, :])
            valid = v * TILE + col_ids < lens[w]
            scores[v, rows, :] = jnp.where(valid, value * score_scale, -1e30)

    def content_pair(column, d):
        content(block(column, 7 - d))
        content(block(column, d + 1))

    tile = 0
    for column, d, h, count in (
        (0, 0, 0, 2),
        (0, 0, 1, 2),
        (1, -1, 0, 1),
        (1, -1, 1, 1),
        (0, 1, 0, 1),
        (0, 1, 1, 2),
        (1, 0, 0, 1),
        (1, 0, 1, 2),
        (0, 2, 0, 1),
        (0, 2, 1, 2),
        (1, 1, 0, 1),
        (1, 1, 1, 1),
    ):
        if d < 0:
            cross_copy(t_cross, h).wait_recv()
            ring_send(1, 0, h)
        else:
            ring_step(column, d, h)
        rel_tiles(tile, tile + count)
        tile += count
    content(t)
    content(t_cross)
    content_pair(0, 0)
    weights_x(0)
    content_pair(1, 0)
    ring_step(1, 2, 0)
    content_pair(0, 1)
    weights_x(1)
    content_pair(0, 2)
    ring_step(1, 2, 1)
    content_pair(1, 1)
    weights_x(2)
    ring_wait(0, 3, 0)
    ring_wait(0, 3, 1)
    content(block(0, 4))
    content_pair(1, 2)
    weights_x(3)
    ring_wait(1, 3, 0)
    ring_wait(1, 3, 1)
    content(block(1, 4))

    peak = jnp.max(scores[...], axis=0)
    peak = jnp.max(peak, axis=-1, keepdims=True)
    gathered = [jnp.zeros((TILE, HD), F32) for _ in range(2)]
    totals = [jnp.zeros((TILE, TILE), F32) for _ in range(2)]
    for v in range(16):
        for w in range(2):
            rows = slice(w * TILE, (w + 1) * TILE)
            weight = jnp.exp(scores[v, rows, :] - peak[rows])
            weight = jnp.where(v * TILE + col_ids < lens[w], weight, 0.0)
            totals[w] = totals[w] + weight
            gathered[w] = gathered[w] + dot_nt(
                weight.astype(BF16), kv[v, HD : 2 * HD, rows]
            )
    heads = [
        (gathered[w] / jnp.sum(totals[w], axis=-1, keepdims=True)).reshape(16, 8, HD)
        for w in range(2)
    ]

    cells = jnp.concatenate(heads, axis=1).astype(BF16)
    for p in range(16):
        hsend[(p // 8) * 2 + p % 2, (p // 2) % 4, :, 0:HD] = cells[p]
    for k in range(1, 4):
        p, dev = g_peer(k)
        rcopy(hsend.at[p], hrecv.at[g], a2a_send, a2a_recv, t, dev).start()
    pltpu.make_async_copy(hsend.at[g], hrecv.at[g], a2a_recv).start()
    bulk_wait(hrecv, a2a_recv)

    def reduce_rows(i, total):
        total = total.reshape(4, 16, D)
        psend[i] = total.astype(BF16)
        for k in (2, 1, 3):
            rcopy(
                psend.at[i, (y + k) % 4], precv.at[i, y], p_send.at[i], p_recv.at[i], t, y_peer(k)
            ).start()
        pown[...] = total
        bulk_wait(precv.at[i, pl.ds(0, 3)], p_recv.at[i])
        result = pown[y]
        for k in range(1, 4):
            result = result + precv[i, (y + k) % 4].astype(F32)
        return result

    weights_end(0)
    total = dot_nn(hrecv[0, :, :, 0:HD].reshape(64, HD), wbuf[0, 0])
    for k in range(1, 4):
        total = total + dot_nn(hrecv[k, :, :, 0:HD].reshape(64, HD), wbuf[0, k])
    pairs = [feat[w, pl.ds(pl.multiple_of((s // 2) * 16, 16), 16), :].astype(F32) for w in range(2)]
    own_rows = jnp.concatenate(
        [jnp.where(core == 0, pair[0:8], pair[8:16]) for pair in pairs], axis=0
    )
    hidden = (own_rows + reduce_rows(0, total)).astype(BF16).astype(F32)
    nbuf[y] = layer_norm(hidden, gains[1:2, :]).astype(BF16)

    for k in (2, 1, 3):
        rcopy(nbuf.at[y], nbuf.at[y], n_send, n_recv, t, y_peer(k)).start()
    weights_end(1)
    weights_end(2)
    bulk_wait(nbuf.at[pl.ds(0, 3)], n_recv)

    rows_all = nbuf[...].reshape(64, D)
    opened = dot_nt(rows_all, wbuf[1].reshape(4 * HD, D))
    gate = dot_nt(rows_all, wbuf[2].reshape(4 * HD, D))
    gated = opened * jax.nn.sigmoid(gate)
    ids = lax.broadcasted_iota(jnp.int32, (64, 4 * HD), 0)
    window = (ids // 8) % 2
    frame = t * TILE + x * 64 + (ids // 16) * 16 + core * 8 + ids % 8
    limit = jnp.where(window == 0, lens[0], lens[1])
    gated = jnp.where(frame < limit, gated, 0.0).astype(BF16)
    gx[core, 1:5] = gated.reshape(4, 16, 4 * HD)

    for cc in range(2):
        rcopy(gx.at[core, 4], gx.at[core, 0], halo_send, halo_recv, t_next, edge[cc]).start()
        rcopy(gx.at[core, 1], gx.at[core, 5], halo_send, halo_recv, t_prev, edge[cc]).start()
    inner = gx.at[core, pl.ds(1, 4)]
    rcopy(inner, inner, halo_send, halo_recv, t, sibling).start()
    bulk_wait(params.at[pl.ds(0, 3)], params_recv)
    taps = jnp.concatenate([params[k, :, 0:HD] for k in range(4)], axis=1)
    bulk_wait(gx.at[:, pl.ds(0, 4)], halo_recv)

    first = jnp.logical_and(t == 0, x == 0)
    last = jnp.logical_and(t == 15, x == 1)
    for cc in range(2):
        for j in range(6):
            block_rows = gx[cc, j].astype(F32)
            if j == 0:
                block_rows = jnp.where(first, 0.0, block_rows)
            if j == 5:
                block_rows = jnp.where(last, 0.0, block_rows)
            start = pl.multiple_of((2 * j + cc + 1 - core) * 8, 8)
            for w in range(2):
                gbuf[w, pl.ds(start, 8), :] = block_rows[w * 8 : w * 8 + 8]
    sums = [jnp.zeros((8, 4 * HD), F32) for _ in range(8)]
    for k in range(31):
        tap = taps[k : k + 1, :]
        for j in range(4):
            for w in range(2):
                row = 16 * j + 9 + k
                sums[2 * j + w] = sums[2 * j + w] + gbuf[w, row : row + 8, :] * tap
    affine = jnp.concatenate(sums, axis=0) * taps[31:32, :] + taps[32:33, :]
    activated = (affine * jax.nn.sigmoid(affine)).astype(BF16)

    weights_end(3)
    total = dot_nn(activated, wbuf[3].reshape(4 * HD, D))
    final = reduce_rows(1, total)
    out[...] = (hidden + final).reshape(2, 8, D).astype(BF16)

    bulk_wait(kv.at[pl.ds(0, 15)], kv_send)
    bulk_wait(wbuf.at[pl.ds(0, 3)], w_send)
    bulk_wait(params.at[pl.ds(0, 3)], params_send)
    bulk_wait(hsend.at[pl.ds(0, 3)], a2a_send)
    for i in range(2):
        bulk_wait(psend.at[i, pl.ds(0, 3)], p_send.at[i])
    bulk_wait(nbuf.at[pl.ds(0, 3)], n_send)
    bulk_wait(gx.at[:, pl.ds(0, 4)], halo_send)


def shards(
    features,
    lengths,
    norm_gains,
    qkv_weight,
    pos_weight,
    pos_biases,
    out_weight,
    conv_in_weight,
    depth_kernel,
    conv_scale,
    conv_shift,
    conv_out_weight,
):
    vmem = pl.BlockSpec(memory_space=pltpu.VMEM)
    hbm = pl.BlockSpec(memory_space=pl.ANY)
    dma = pltpu.SemaphoreType.DMA
    return pl.pallas_call(
        kernel,
        out_shape=jax.ShapeDtypeStruct((2, 8, D), BF16),
        in_specs=[pl.BlockSpec(memory_space=pltpu.SMEM)] + [vmem] * 3 + [hbm, vmem, hbm, hbm] + [vmem] * 3 + [hbm],
        out_specs=vmem,
        scratch_shapes=[
            pltpu.VMEM((256, D), BF16),
            pltpu.VMEM((16, 2 * HD, 256), BF16),
            pltpu.VMEM((256, HD), BF16),
            pltpu.VMEM((256, HD), BF16),
            pltpu.VMEM((TILE, HALF), F32),
            pltpu.VMEM((TILE, HALF), F32),
            pltpu.VMEM((24, HALF), F32),
            pltpu.VMEM((24, HALF), F32),
            pltpu.VMEM((17, 256, TILE), F32),
            pltpu.VMEM((16, 256, TILE), F32),
            pltpu.VMEM((4, 4, HD, D), BF16),
            pltpu.VMEM((4, 40, TILE), F32),
            pltpu.VMEM((4, 4, 16, TILE), BF16),
            pltpu.VMEM((4, 4, 16, TILE), BF16),
            pltpu.VMEM((2, 4, 16, D), BF16),
            pltpu.VMEM((2, 4, 16, D), BF16),
            pltpu.VMEM((4, 16, D), F32),
            pltpu.VMEM((4, 16, D), BF16),
            pltpu.VMEM((2, 6, 16, 4 * HD), BF16),
            pltpu.VMEM((2, 112, 4 * HD), F32),
            dma,
            dma((2, 2, 4, 2)),
            dma((2,)),
            dma,
            dma((4,)),
            dma((4,)),
            dma((4,)),
            dma,
            dma,
            dma((2,)),
            dma((2,)),
            dma,
            dma,
            dma,
            dma,
            dma,
            dma,
            pltpu.VMEM((HD, D), BF16),
            dma,
        ],
        compiler_params=pltpu.CompilerParams(
            collective_id=0, has_side_effects=True, vmem_limit_bytes=60 * 2**20
        ),
    )(
        lengths,
        features,
        norm_gains,
        qkv_weight,
        pos_weight,
        pos_biases,
        out_weight,
        conv_in_weight,
        depth_kernel,
        conv_scale.reshape(1, HD),
        conv_shift.reshape(1, HD),
        conv_out_weight,
    )


def solution(mesh):
    return jax.shard_map(
        shards,
        mesh=mesh,
        in_specs=(
            P(None, "tm", None),
            P(),
            P(),
            P(None, "tensor", None),
            P("tensor", None),
            P(None, "tensor"),
            P("tensor", None),
            P(None, "tensor", None),
            P(None, "tensor"),
            P("tensor"),
            P("tensor"),
            P("tensor", None),
        ),
        out_specs=P(None, ("tm", "tensor"), None),
        check_vma=False,
    )
```

```python
import math

import jax
import jax.numpy as jnp
from jax import lax
from jax.experimental import pallas as pl
from jax.experimental.pallas import tpu as pltpu
from jax.sharding import PartitionSpec as P

MESH = pl.DeviceIdType.MESH
HD = 96
D = 1536
HALF = D // 2
TILE = 128
EPS = 1e-05
F32 = jnp.float32
BF16 = jnp.bfloat16


def layer_norm(values, gain):
    row_mean = jnp.mean(values, axis=-1, keepdims=True)
    centred = values - row_mean
    variance = jnp.mean(centred * centred, axis=-1, keepdims=True)
    return centred * lax.rsqrt(variance + EPS) * gain


def dot_nt(a, b):
    return lax.dot_general(a, b, (((1,), (1,)), ((), ())), preferred_element_type=F32)


def dot_nn(a, b):
    return jnp.dot(a, b, preferred_element_type=F32)


def rcopy(src, dst, send_sem, recv_sem, tm, tensor):
    return pltpu.make_async_remote_copy(
        src_ref=src,
        dst_ref=dst,
        send_sem=send_sem,
        recv_sem=recv_sem,
        device_id=(tm, tensor),
        device_id_type=MESH,
    )


def bulk_wait(ref, sem):
    pltpu.make_async_copy(ref, ref, sem).wait()


def kernel(
    lens,
    feat,
    gains,
    wqkv,
    wpos_in,
    pbias,
    wout,
    wcin,
    dker,
    cscale,
    cshift,
    wcout,
    out,
    normed,
    kv,
    q_content,
    q_position,
    fine_sin,
    fine_cos,
    coarse_sin,
    coarse_cos,
    rot,
    scores,
    wbuf,
    params,
    hsend,
    hrecv,
    psend,
    precv,
    pown,
    nbuf,
    gx,
    gbuf,
    kv_send,
    ring_recv,
    cross_recv,
    w_send,
    wx_recv,
    ws_recv,
    w_local,
    a2a_send,
    a2a_recv,
    p_send,
    p_recv,
    n_send,
    n_recv,
    halo_send,
    halo_recv,
    params_send,
    params_recv,
    wpos,
    wpos_sem,
    relay,
):
    t = lax.axis_index("tm")
    s = lax.axis_index("tensor")
    z = t % 8
    base = (t // 8) * 8
    other = 8 - base
    z_right = base + (z + 1) % 8
    z_left = base + (z + 7) % 8
    t_cross = (t + 8) % 16
    core = s % 2
    y = (s // 2) % 4
    x = s // 8
    g = x * 2 + core
    sibling = s + 1 - 2 * core
    s_cross = (s + 8) % 16
    g_cross = (1 - x) * 2 + core
    t_next = (t + x) % 16
    t_prev = (t + 15 + x) % 16
    edge = [(1 - x) * 8 + y * 2 + cc for cc in range(2)]

    def y_peer(k):
        return x * 8 + ((y + k) % 4) * 2 + core

    def g_peer(k):
        p = (g + k) % 4
        return p, (p // 2) * 8 + y * 2 + p % 2

    score_scale = 1.0 / math.sqrt(HD)

    barrier = pltpu.get_barrier_semaphore()
    peers = [(t, y_peer(k)) for k in range(1, 4)]
    peers += [(t, g_peer(k)[1]) for k in range(1, 4)]
    peers += [(t_cross, s_cross), (t_cross, s), (z_right, s), (z_left, s)]
    peers += [(t_next, p) for p in edge] + [(t_prev, p) for p in edge]
    for peer in peers:
        pl.semaphore_signal(barrier, inc=1, device_id=peer, device_id_type=MESH)

    wpos_copy = pltpu.make_async_copy(wpos_in, wpos, wpos_sem)
    wpos_copy.start()

    params[g, 0:31, 0:HD] = dker[...]
    params[g, 31:32, 0:HD] = cscale[...]
    params[g, 32:33, 0:HD] = cshift[...]

    gain_one = gains[0:1, :]
    for w in range(2):

        @pl.loop(0, 8, unroll=2)
        def _(i, w=w):
            rows = feat[w, pl.ds(pl.multiple_of(i * 16, 16), 16), :].astype(F32)
            normed[pl.ds(pl.multiple_of(w * TILE + i * 16, 16), 16), :] = layer_norm(
                rows, gain_one
            ).astype(BF16)

    kv[t] = dot_nt(wqkv[1:3].reshape(2 * HD, D), normed[...]).astype(BF16)

    pl.semaphore_wait(barrier, len(peers))

    def block(column, offset):
        return (base if column == 0 else other) + (z + offset) % 8

    def ring_copy(v, way, column, d, h):
        ref = kv.at[v, pl.ds(HD * h, HD)]
        return rcopy(
            ref,
            ref,
            kv_send,
            ring_recv.at[way, column, d, h],
            z_right if way == 0 else z_left,
            s,
        )

    def ring_send(column, d, h):
        for way in range(2):
            if d < 3 or h == way:
                ring_copy(block(column, 8 - d if way == 0 else d), way, column, d, h).start()

    def ring_wait(column, d, h):
        for way in range(2):
            if d < 3 or h == way:
                v = block(column, 7 - d if way == 0 else d + 1)
                ring_copy(v, way, column, d, h).wait_recv()

    def ring_step(column, d, h):
        ring_wait(column, d, h)
        ring_send(column, d + 1, h)

    def cross_copy(v, h):
        ref = kv.at[v, pl.ds(HD * h, HD)]
        return rcopy(ref, ref, kv_send, cross_recv.at[h], t_cross, s)

    own_weights = [wout, wcin.at[0], wcin.at[1], wcout]

    def weights_start(m):
        own = own_weights[m]
        for half, tm in ((0, t), (1, t_cross)):
            rows = pl.ds(48 * half, 48)
            rcopy(
                own.at[rows], wbuf.at[m, g, rows], w_send, wx_recv.at[m], tm, s_cross
            ).start()
        rcopy(own, wbuf.at[m, g], w_send, ws_recv.at[m], t, sibling).start()
        pltpu.make_async_copy(own, wbuf.at[m, g], w_local.at[m]).start()

    def weights_x(m):
        ref = wbuf.at[m, g_cross]
        bulk_wait(ref, wx_recv.at[m])
        rcopy(ref, ref, w_send, ws_recv.at[m], t, sibling).start()

    def weights_end(m):
        bulk_wait(wbuf.at[m, pl.ds(0, 2)], ws_recv.at[m])
        pltpu.make_async_copy(own_weights[m], wbuf.at[m, g], w_local.at[m]).wait()

    for h in range(2):
        ring_send(0, 0, h)
        cross_copy(t, h).start()
    for m in range(4):
        weights_start(m)
    for k in range(1, 4):
        rcopy(
            params.at[g], params.at[g], params_send, params_recv, t, g_peer(k)[1]
        ).start()

    query = dot_nt(normed[...], wqkv[0])
    q_content[...] = (query + pbias[0:1, :]).astype(BF16)
    q_position[...] = (query + pbias[1:2, :]).astype(BF16)
    wpos_copy.wait()
    frequency = jnp.exp(
        lax.broadcasted_iota(jnp.int32, (1, HALF), 1).astype(F32)
        * (-2.0 * math.log(10000.0) / D)
    )

    n_ids = lax.broadcasted_iota(jnp.int32, (24, 1), 0)
    coarse = ((t - n_ids) * TILE).astype(F32) * frequency
    coarse_sin[...] = jnp.sin(coarse)
    coarse_cos[...] = jnp.cos(coarse)

    @pl.loop(0, 8)
    def _(i):
        ids = 127 - i * 16 - lax.broadcasted_iota(jnp.int32, (16, 1), 0)
        angle = ids.astype(F32) * frequency
        rows = pl.ds(pl.multiple_of(i * 16, 16), 16)
        fine_sin[rows, :] = jnp.sin(angle)
        fine_cos[rows, :] = jnp.cos(angle)

    def rel_tiles(start, stop):
        @pl.loop(start, stop)
        def _(n):
            a_sin = coarse_sin[pl.ds(n, 1), :]
            a_cos = coarse_cos[pl.ds(n, 1), :]
            f_sin = fine_sin[...]
            f_cos = fine_cos[...]
            pe_sin = (a_sin * f_cos + a_cos * f_sin).astype(BF16)
            pe_cos = (a_cos * f_cos - a_sin * f_sin).astype(BF16)
            rel = dot_nt(wpos[:, 0:HALF], pe_sin) + dot_nt(wpos[:, HALF:D], pe_cos)
            part_scores = dot_nn(q_position[...], rel.astype(BF16))
            for w in range(2):
                rot[n, pl.ds(w * TILE, TILE), :] = pltpu.roll(
                    part_scores[w * TILE : (w + 1) * TILE],
                    1,
                    1,
                    stride=1,
                    stride_axis=0,
                )

    row_ids = lax.broadcasted_iota(jnp.int32, (TILE, TILE), 0)
    col_ids = lax.broadcasted_iota(jnp.int32, (TILE, TILE), 1)

    def content(v):
        for w in range(2):
            rows = pl.ds(w * TILE, TILE)
            value = dot_nn(q_content[rows, :], kv[v, 0:HD, pl.ds(w * TILE, TILE)])
            value = value + jnp.where(col_ids <= row_ids, rot[v, rows, :], rot[v + 1, rows, :])
            valid = v * TILE + col_ids < lens[w]
            scores[v, rows, :] = jnp.where(valid, value * score_scale, -1e30)

    def content_pair(column, d):
        content(block(column, 7 - d))
        content(block(column, d + 1))

    tile = 0
    for column, d, h, count in (
        (0, 0, 0, 2),
        (0, 0, 1, 2),
        (1, -1, 0, 1),
        (1, -1, 1, 1),
        (0, 1, 0, 1),
        (0, 1, 1, 2),
        (1, 0, 0, 1),
        (1, 0, 1, 2),
        (0, 2, 0, 1),
        (0, 2, 1, 2),
        (1, 1, 0, 1),
        (1, 1, 1, 1),
    ):
        if d < 0:
            cross_copy(t_cross, h).wait_recv()
            ring_send(1, 0, h)
        else:
            ring_step(column, d, h)
        rel_tiles(tile, tile + count)
        tile += count
    content(t)
    content(t_cross)
    content_pair(0, 0)
    weights_x(0)
    content_pair(1, 0)
    ring_step(1, 2, 0)
    content_pair(0, 1)
    weights_x(1)
    content_pair(0, 2)
    ring_step(1, 2, 1)
    content_pair(1, 1)
    weights_x(2)
    ring_wait(0, 3, 0)
    ring_wait(0, 3, 1)
    content(block(0, 4))
    content_pair(1, 2)
    weights_x(3)
    ring_wait(1, 3, 0)
    ring_wait(1, 3, 1)
    content(block(1, 4))

    peak = jnp.max(scores[...], axis=0)
    peak = jnp.max(peak, axis=-1, keepdims=True)
    gathered = [jnp.zeros((TILE, HD), F32) for _ in range(2)]
    totals = [jnp.zeros((TILE, TILE), F32) for _ in range(2)]
    for v in range(16):
        for w in range(2):
            rows = slice(w * TILE, (w + 1) * TILE)
            weight = jnp.exp(scores[v, rows, :] - peak[rows])
            weight = jnp.where(v * TILE + col_ids < lens[w], weight, 0.0)
            totals[w] = totals[w] + weight
            gathered[w] = gathered[w] + dot_nt(
                weight.astype(BF16), kv[v, HD : 2 * HD, rows]
            )
    heads = [
        (gathered[w] / jnp.sum(totals[w], axis=-1, keepdims=True)).reshape(16, 8, HD)
        for w in range(2)
    ]

    cells = jnp.concatenate(heads, axis=1).astype(BF16)
    for p in range(16):
        hsend[(p // 8) * 2 + p % 2, (p // 2) % 4, :, 0:HD] = cells[p]
    for k in range(1, 4):
        p, dev = g_peer(k)
        rcopy(hsend.at[p], hrecv.at[g], a2a_send, a2a_recv, t, dev).start()
    pltpu.make_async_copy(hsend.at[g], hrecv.at[g], a2a_recv).start()
    bulk_wait(hrecv, a2a_recv)

    def reduce_rows(i, total):
        total = total.reshape(4, 16, D)
        psend[i] = total.astype(BF16)
        def hop(src, dst, sem, k):
            return rcopy(src, dst, p_send.at[i], p_recv.at[i, sem], t, y_peer(k))

        left, right, far = (y + 3) % 4, (y + 1) % 4, (y + 2) % 4
        halves = [pl.ds(0, HALF), pl.ds(HALF, HALF)]
        for h, k in ((0, 1), (1, 3)):
            hop(psend.at[i, far, :, halves[h]], relay.at[i, h], h, k).start()
        hop(psend.at[i, right], precv.at[i, y], 2, 1).start()
        hop(psend.at[i, left], precv.at[i, y], 3, 3).start()
        pown[...] = total
        for h, k, origin in ((0, 1, left), (1, 3, right)):
            bulk_wait(relay.at[i, h], p_recv.at[i, h])
            hop(relay.at[i, h], precv.at[i, origin, :, halves[h]], 4 + h, k).start()
        bulk_wait(precv.at[i, left], p_recv.at[i, 2])
        bulk_wait(precv.at[i, right], p_recv.at[i, 3])
        for h in range(2):
            bulk_wait(precv.at[i, far, :, halves[h]], p_recv.at[i, 4 + h])
        result = pown[y]
        for k in range(1, 4):
            result = result + precv[i, (y + k) % 4].astype(F32)
        return result

    weights_end(0)
    total = dot_nn(hrecv[0, :, :, 0:HD].reshape(64, HD), wbuf[0, 0])
    for k in range(1, 4):
        total = total + dot_nn(hrecv[k, :, :, 0:HD].reshape(64, HD), wbuf[0, k])
    pairs = [feat[w, pl.ds(pl.multiple_of((s // 2) * 16, 16), 16), :].astype(F32) for w in range(2)]
    own_rows = jnp.concatenate(
        [jnp.where(core == 0, pair[0:8], pair[8:16]) for pair in pairs], axis=0
    )
    hidden = (own_rows + reduce_rows(0, total)).astype(BF16).astype(F32)
    nbuf[y] = layer_norm(hidden, gains[1:2, :]).astype(BF16)

    def n_copy(p, h, sem, k):
        ref = nbuf.at[p, :, pl.ds(HALF * h, HALF)]
        return rcopy(ref, ref, n_send, n_recv.at[sem], t, y_peer(k))

    left, right, far = (y + 3) % 4, (y + 1) % 4, (y + 2) % 4
    n_copy(y, 0, 0, 1).start()
    n_copy(y, 1, 3, 3).start()
    n_copy(y, 1, 1, 1).start()
    n_copy(y, 0, 2, 3).start()
    n_copy(left, 0, 0, 1).wait_recv()
    n_copy(left, 0, 4, 1).start()
    n_copy(right, 1, 3, 3).wait_recv()
    n_copy(right, 1, 5, 3).start()
    weights_end(1)
    weights_end(2)
    n_copy(left, 1, 1, 1).wait_recv()
    n_copy(right, 0, 2, 3).wait_recv()
    n_copy(far, 0, 4, 1).wait_recv()
    n_copy(far, 1, 5, 3).wait_recv()

    rows_all = nbuf[...].reshape(64, D)
    opened = dot_nt(rows_all, wbuf[1].reshape(4 * HD, D))
    gate = dot_nt(rows_all, wbuf[2].reshape(4 * HD, D))
    gated = opened * jax.nn.sigmoid(gate)
    ids = lax.broadcasted_iota(jnp.int32, (64, 4 * HD), 0)
    window = (ids // 8) % 2
    frame = t * TILE + x * 64 + (ids // 16) * 16 + core * 8 + ids % 8
    limit = jnp.where(window == 0, lens[0], lens[1])
    gated = jnp.where(frame < limit, gated, 0.0).astype(BF16)
    gx[core, 1:5] = gated.reshape(4, 16, 4 * HD)

    for cc in range(2):
        rcopy(gx.at[core, 4], gx.at[core, 0], halo_send, halo_recv, t_next, edge[cc]).start()
        rcopy(gx.at[core, 1], gx.at[core, 5], halo_send, halo_recv, t_prev, edge[cc]).start()
    inner = gx.at[core, pl.ds(1, 4)]
    rcopy(inner, inner, halo_send, halo_recv, t, sibling).start()
    bulk_wait(params.at[pl.ds(0, 3)], params_recv)
    taps = jnp.concatenate([params[k, :, 0:HD] for k in range(4)], axis=1)
    bulk_wait(gx.at[:, pl.ds(0, 4)], halo_recv)

    first = jnp.logical_and(t == 0, x == 0)
    last = jnp.logical_and(t == 15, x == 1)
    for cc in range(2):
        for j in range(6):
            block_rows = gx[cc, j].astype(F32)
            if j == 0:
                block_rows = jnp.where(first, 0.0, block_rows)
            if j == 5:
                block_rows = jnp.where(last, 0.0, block_rows)
            start = pl.multiple_of((2 * j + cc + 1 - core) * 8, 8)
            for w in range(2):
                gbuf[w, pl.ds(start, 8), :] = block_rows[w * 8 : w * 8 + 8]
    sums = [jnp.zeros((8, 4 * HD), F32) for _ in range(8)]
    for k in range(31):
        tap = taps[k : k + 1, :]
        for j in range(4):
            for w in range(2):
                row = 16 * j + 9 + k
                sums[2 * j + w] = sums[2 * j + w] + gbuf[w, row : row + 8, :] * tap
    affine = jnp.concatenate(sums, axis=0) * taps[31:32, :] + taps[32:33, :]
    activated = (affine * jax.nn.sigmoid(affine)).astype(BF16)

    weights_end(3)
    total = dot_nn(activated, wbuf[3].reshape(4 * HD, D))
    final = reduce_rows(1, total)
    out[...] = (hidden + final).reshape(2, 8, D).astype(BF16)

    bulk_wait(kv.at[pl.ds(0, 15)], kv_send)
    bulk_wait(wbuf.at[pl.ds(0, 3)], w_send)
    bulk_wait(params.at[pl.ds(0, 3)], params_send)
    bulk_wait(hsend.at[pl.ds(0, 3)], a2a_send)
    for i in range(2):
        bulk_wait(psend.at[i], p_send.at[i])
    bulk_wait(nbuf.at[pl.ds(0, 3)], n_send)
    bulk_wait(gx.at[:, pl.ds(0, 4)], halo_send)


def shards(
    features,
    lengths,
    norm_gains,
    qkv_weight,
    pos_weight,
    pos_biases,
    out_weight,
    conv_in_weight,
    depth_kernel,
    conv_scale,
    conv_shift,
    conv_out_weight,
):
    vmem = pl.BlockSpec(memory_space=pltpu.VMEM)
    hbm = pl.BlockSpec(memory_space=pl.ANY)
    dma = pltpu.SemaphoreType.DMA
    return pl.pallas_call(
        kernel,
        out_shape=jax.ShapeDtypeStruct((2, 8, D), BF16),
        in_specs=[pl.BlockSpec(memory_space=pltpu.SMEM)] + [vmem] * 3 + [hbm, vmem, hbm, hbm] + [vmem] * 3 + [hbm],
        out_specs=vmem,
        scratch_shapes=[
            pltpu.VMEM((256, D), BF16),
            pltpu.VMEM((16, 2 * HD, 256), BF16),
            pltpu.VMEM((256, HD), BF16),
            pltpu.VMEM((256, HD), BF16),
            pltpu.VMEM((TILE, HALF), F32),
            pltpu.VMEM((TILE, HALF), F32),
            pltpu.VMEM((24, HALF), F32),
            pltpu.VMEM((24, HALF), F32),
            pltpu.VMEM((17, 256, TILE), F32),
            pltpu.VMEM((16, 256, TILE), F32),
            pltpu.VMEM((4, 4, HD, D), BF16),
            pltpu.VMEM((4, 40, TILE), F32),
            pltpu.VMEM((4, 4, 16, TILE), BF16),
            pltpu.VMEM((4, 4, 16, TILE), BF16),
            pltpu.VMEM((2, 4, 16, D), BF16),
            pltpu.VMEM((2, 4, 16, D), BF16),
            pltpu.VMEM((4, 16, D), F32),
            pltpu.VMEM((4, 16, D), BF16),
            pltpu.VMEM((2, 6, 16, 4 * HD), BF16),
            pltpu.VMEM((2, 112, 4 * HD), F32),
            dma,
            dma((2, 2, 4, 2)),
            dma((2,)),
            dma,
            dma((4,)),
            dma((4,)),
            dma((4,)),
            dma,
            dma,
            dma((2,)),
            dma((2, 6)),
            dma,
            dma((6,)),
            dma,
            dma,
            dma,
            dma,
            pltpu.VMEM((HD, D), BF16),
            dma,
            pltpu.VMEM((2, 2, 16, HALF), BF16),
        ],
        compiler_params=pltpu.CompilerParams(
            collective_id=0, has_side_effects=True, vmem_limit_bytes=60 * 2**20
        ),
    )(
        lengths,
        features,
        norm_gains,
        qkv_weight,
        pos_weight,
        pos_biases,
        out_weight,
        conv_in_weight,
        depth_kernel,
        conv_scale.reshape(1, HD),
        conv_shift.reshape(1, HD),
        conv_out_weight,
    )


def solution(mesh):
    return jax.shard_map(
        shards,
        mesh=mesh,
        in_specs=(
            P(None, "tm", None),
            P(),
            P(),
            P(None, "tensor", None),
            P("tensor", None),
            P(None, "tensor"),
            P("tensor", None),
            P(None, "tensor", None),
            P(None, "tensor"),
            P("tensor"),
            P("tensor"),
            P("tensor", None),
        ),
        out_specs=P(None, ("tm", "tensor"), None),
        check_vma=False,
    )
```

```python
import math

import jax
import jax.numpy as jnp
from jax import lax
from jax.experimental import pallas as pl
from jax.experimental.pallas import tpu as pltpu
from jax.sharding import PartitionSpec as P

MESH = pl.DeviceIdType.MESH
HD = 96
D = 1536
HALF = D // 2
TILE = 128
EPS = 1e-05
F32 = jnp.float32
BF16 = jnp.bfloat16


def layer_norm(values, gain):
    row_mean = jnp.mean(values, axis=-1, keepdims=True)
    centred = values - row_mean
    variance = jnp.mean(centred * centred, axis=-1, keepdims=True)
    return centred * lax.rsqrt(variance + EPS) * gain


def dot_nt(a, b):
    return lax.dot_general(a, b, (((1,), (1,)), ((), ())), preferred_element_type=F32)


def dot_nn(a, b):
    return jnp.dot(a, b, preferred_element_type=F32)


def rcopy(src, dst, send_sem, recv_sem, tm, tensor):
    return pltpu.make_async_remote_copy(
        src_ref=src,
        dst_ref=dst,
        send_sem=send_sem,
        recv_sem=recv_sem,
        device_id=(tm, tensor),
        device_id_type=MESH,
    )


def bulk_wait(ref, sem):
    pltpu.make_async_copy(ref, ref, sem).wait()


def kernel(
    lens,
    feat,
    gains,
    wqkv,
    wpos_in,
    pbias,
    wout,
    wcin,
    dker,
    cscale,
    cshift,
    wcout,
    out,
    normed,
    kv,
    q_content,
    q_position,
    fine_sin,
    fine_cos,
    coarse_sin,
    coarse_cos,
    rot,
    scores,
    wbuf,
    params,
    hsend,
    hrecv,
    psend,
    precv,
    pown,
    nbuf,
    gx,
    gbuf,
    kv_send,
    ring_recv,
    cross_recv,
    w_send,
    wx_recv,
    ws_recv,
    w_local,
    a2a_send,
    a2a_recv,
    p_send,
    p_recv,
    n_send,
    n_recv,
    halo_send,
    halo_recv,
    params_send,
    params_recv,
    wpos,
    wpos_sem,
):
    t = lax.axis_index("tm")
    s = lax.axis_index("tensor")
    z = t % 8
    base = (t // 8) * 8
    other = 8 - base
    z_right = base + (z + 1) % 8
    z_left = base + (z + 7) % 8
    t_cross = (t + 8) % 16
    core = s % 2
    y = (s // 2) % 4
    x = s // 8
    g = x * 2 + core
    sibling = s + 1 - 2 * core
    s_cross = (s + 8) % 16
    g_cross = (1 - x) * 2 + core
    t_next = (t + x) % 16
    t_prev = (t + 15 + x) % 16
    edge = [(1 - x) * 8 + y * 2 + cc for cc in range(2)]

    def y_peer(k):
        return x * 8 + ((y + k) % 4) * 2 + core

    def g_peer(k):
        p = (g + k) % 4
        return p, (p // 2) * 8 + y * 2 + p % 2

    score_scale = 1.0 / math.sqrt(HD)

    barrier = pltpu.get_barrier_semaphore()
    peers = [(t, y_peer(k)) for k in range(1, 4)]
    peers += [(t, g_peer(k)[1]) for k in range(1, 4)]
    peers += [(t_cross, s_cross), (t_cross, s), (z_right, s), (z_left, s)]
    peers += [(t_next, p) for p in edge] + [(t_prev, p) for p in edge]
    for peer in peers:
        pl.semaphore_signal(barrier, inc=1, device_id=peer, device_id_type=MESH)

    wpos_copy = pltpu.make_async_copy(wpos_in, wpos, wpos_sem)
    wpos_copy.start()

    params[g, 0:31, 0:HD] = dker[...]
    params[g, 31:32, 0:HD] = cscale[...]
    params[g, 32:33, 0:HD] = cshift[...]

    gain_one = gains[0:1, :]
    for w in range(2):

        @pl.loop(0, 8, unroll=4)
        def _(i, w=w):
            rows = feat[w, pl.ds(pl.multiple_of(i * 16, 16), 16), :].astype(F32)
            normed[pl.ds(pl.multiple_of(w * TILE + i * 16, 16), 16), :] = layer_norm(
                rows, gain_one
            ).astype(BF16)

    kv[t] = dot_nt(wqkv[1:3].reshape(2 * HD, D), normed[...]).astype(BF16)

    pl.semaphore_wait(barrier, len(peers))

    def block(column, offset):
        return (base if column == 0 else other) + (z + offset) % 8

    def ring_copy(v, way, column, d, h):
        ref = kv.at[v, pl.ds(HD * h, HD)]
        return rcopy(
            ref,
            ref,
            kv_send,
            ring_recv.at[way, column, d, h],
            z_right if way == 0 else z_left,
            s,
        )

    def ring_send(column, d, h):
        for way in range(2):
            if d < 3 or h == way:
                ring_copy(block(column, 8 - d if way == 0 else d), way, column, d, h).start()

    def ring_wait(column, d, h):
        for way in range(2):
            if d < 3 or h == way:
                v = block(column, 7 - d if way == 0 else d + 1)
                ring_copy(v, way, column, d, h).wait_recv()

    def ring_step(column, d, h):
        ring_wait(column, d, h)
        ring_send(column, d + 1, h)

    def cross_copy(v, h):
        ref = kv.at[v, pl.ds(HD * h, HD)]
        return rcopy(ref, ref, kv_send, cross_recv.at[h], t_cross, s)

    own_weights = [wout, wcin.at[0], wcin.at[1], wcout]

    def weights_start(m):
        own = own_weights[m]
        for half, tm in ((0, t), (1, t_cross)):
            rows = pl.ds(48 * half, 48)
            rcopy(
                own.at[rows], wbuf.at[m, g, rows], w_send, wx_recv.at[m], tm, s_cross
            ).start()
        rcopy(own, wbuf.at[m, g], w_send, ws_recv.at[m], t, sibling).start()
        pltpu.make_async_copy(own, wbuf.at[m, g], w_local.at[m]).start()

    def weights_x(m):
        ref = wbuf.at[m, g_cross]
        bulk_wait(ref, wx_recv.at[m])
        rcopy(ref, ref, w_send, ws_recv.at[m], t, sibling).start()

    def weights_end(m):
        bulk_wait(wbuf.at[m, pl.ds(0, 2)], ws_recv.at[m])
        pltpu.make_async_copy(own_weights[m], wbuf.at[m, g], w_local.at[m]).wait()

    for h in range(2):
        ring_send(0, 0, h)
        cross_copy(t, h).start()
    for m in range(4):
        weights_start(m)
    for k in range(1, 4):
        rcopy(
            params.at[g], params.at[g], params_send, params_recv, t, g_peer(k)[1]
        ).start()

    query = dot_nt(normed[...], wqkv[0])
    q_content[...] = (query + pbias[0:1, :]).astype(BF16)
    q_position[...] = (query + pbias[1:2, :]).astype(BF16)
    wpos_copy.wait()
    frequency = jnp.exp(
        lax.broadcasted_iota(jnp.int32, (1, HALF), 1).astype(F32)
        * (-2.0 * math.log(10000.0) / D)
    )

    n_ids = lax.broadcasted_iota(jnp.int32, (24, 1), 0)
    coarse = ((t - n_ids) * TILE).astype(F32) * frequency
    coarse_sin[...] = jnp.sin(coarse)
    coarse_cos[...] = jnp.cos(coarse)

    @pl.loop(0, 8)
    def _(i):
        ids = 127 - i * 16 - lax.broadcasted_iota(jnp.int32, (16, 1), 0)
        angle = ids.astype(F32) * frequency
        rows = pl.ds(pl.multiple_of(i * 16, 16), 16)
        fine_sin[rows, :] = jnp.sin(angle)
        fine_cos[rows, :] = jnp.cos(angle)

    def rel_tiles(start, stop):
        @pl.loop(start, stop)
        def _(n):
            a_sin = coarse_sin[pl.ds(n, 1), :]
            a_cos = coarse_cos[pl.ds(n, 1), :]
            f_sin = fine_sin[...]
            f_cos = fine_cos[...]
            pe_sin = (a_sin * f_cos + a_cos * f_sin).astype(BF16)
            pe_cos = (a_cos * f_cos - a_sin * f_sin).astype(BF16)
            rel = dot_nt(wpos[:, 0:HALF], pe_sin) + dot_nt(wpos[:, HALF:D], pe_cos)
            part_scores = dot_nn(q_position[...], rel.astype(BF16))
            for w in range(2):
                rot[n, pl.ds(w * TILE, TILE), :] = pltpu.roll(
                    part_scores[w * TILE : (w + 1) * TILE],
                    1,
                    1,
                    stride=1,
                    stride_axis=0,
                )

    row_ids = lax.broadcasted_iota(jnp.int32, (TILE, TILE), 0)
    col_ids = lax.broadcasted_iota(jnp.int32, (TILE, TILE), 1)

    def content(v):
        for w in range(2):
            rows = pl.ds(w * TILE, TILE)
            value = dot_nn(q_content[rows, :], kv[v, 0:HD, pl.ds(w * TILE, TILE)])
            value = value + jnp.where(col_ids <= row_ids, rot[v, rows, :], rot[v + 1, rows, :])
            valid = v * TILE + col_ids < lens[w]
            scores[v, rows, :] = jnp.where(valid, value * score_scale, -1e30)

    def content_pair(column, d):
        content(block(column, 7 - d))
        content(block(column, d + 1))

    tile = 0
    for column, d, h, count in (
        (0, 0, 0, 2),
        (0, 0, 1, 2),
        (1, -1, 0, 1),
        (1, -1, 1, 1),
        (0, 1, 0, 1),
        (0, 1, 1, 2),
        (1, 0, 0, 1),
        (1, 0, 1, 2),
        (0, 2, 0, 1),
        (0, 2, 1, 2),
        (1, 1, 0, 1),
        (1, 1, 1, 1),
    ):
        if d < 0:
            cross_copy(t_cross, h).wait_recv()
            ring_send(1, 0, h)
        else:
            ring_step(column, d, h)
        rel_tiles(tile, tile + count)
        tile += count
    content(t)
    content(t_cross)
    content_pair(0, 0)
    weights_x(0)
    content_pair(1, 0)
    ring_step(1, 2, 0)
    content_pair(0, 1)
    weights_x(1)
    content_pair(0, 2)
    ring_step(1, 2, 1)
    content_pair(1, 1)
    weights_x(2)
    ring_wait(0, 3, 0)
    ring_wait(0, 3, 1)
    content(block(0, 4))
    content_pair(1, 2)
    weights_x(3)
    ring_wait(1, 3, 0)
    ring_wait(1, 3, 1)
    content(block(1, 4))

    peak = jnp.max(scores[...], axis=0)
    peak = jnp.max(peak, axis=-1, keepdims=True)
    gathered = [jnp.zeros((TILE, HD), F32) for _ in range(2)]
    totals = [jnp.zeros((TILE, TILE), F32) for _ in range(2)]
    for v in range(16):
        for w in range(2):
            rows = slice(w * TILE, (w + 1) * TILE)
            weight = jnp.exp(scores[v, rows, :] - peak[rows])
            weight = jnp.where(v * TILE + col_ids < lens[w], weight, 0.0)
            totals[w] = totals[w] + weight
            gathered[w] = gathered[w] + dot_nt(
                weight.astype(BF16), kv[v, HD : 2 * HD, rows]
            )
    heads = [
        (gathered[w] / jnp.sum(totals[w], axis=-1, keepdims=True)).reshape(16, 8, HD)
        for w in range(2)
    ]

    cells = jnp.concatenate(heads, axis=1).astype(BF16)
    for p in range(16):
        hsend[(p // 8) * 2 + p % 2, (p // 2) % 4, :, 0:HD] = cells[p]
    for k in range(1, 4):
        p, dev = g_peer(k)
        rcopy(hsend.at[p], hrecv.at[g], a2a_send, a2a_recv, t, dev).start()
    pltpu.make_async_copy(hsend.at[g], hrecv.at[g], a2a_recv).start()
    bulk_wait(hrecv, a2a_recv)

    def reduce_rows(i, total):
        total = total.reshape(4, 16, D)
        psend[i] = total.astype(BF16)
        for k in (2, 1, 3):
            rcopy(
                psend.at[i, (y + k) % 4], precv.at[i, y], p_send.at[i], p_recv.at[i], t, y_peer(k)
            ).start()
        pown[...] = total
        bulk_wait(precv.at[i, pl.ds(0, 3)], p_recv.at[i])
        result = pown[y]
        for k in range(1, 4):
            result = result + precv[i, (y + k) % 4].astype(F32)
        return result

    weights_end(0)
    total = dot_nn(hrecv[0, :, :, 0:HD].reshape(64, HD), wbuf[0, 0])
    for k in range(1, 4):
        total = total + dot_nn(hrecv[k, :, :, 0:HD].reshape(64, HD), wbuf[0, k])
    pairs = [feat[w, pl.ds(pl.multiple_of((s // 2) * 16, 16), 16), :].astype(F32) for w in range(2)]
    own_rows = jnp.concatenate(
        [jnp.where(core == 0, pair[0:8], pair[8:16]) for pair in pairs], axis=0
    )
    hidden = (own_rows + reduce_rows(0, total)).astype(BF16).astype(F32)
    nbuf[y] = layer_norm(hidden, gains[1:2, :]).astype(BF16)

    for k in (2, 1, 3):
        rcopy(nbuf.at[y], nbuf.at[y], n_send, n_recv, t, y_peer(k)).start()
    weights_end(1)
    weights_end(2)
    bulk_wait(nbuf.at[pl.ds(0, 3)], n_recv)

    rows_all = nbuf[...].reshape(64, D)
    opened = dot_nt(rows_all, wbuf[1].reshape(4 * HD, D))
    gate = dot_nt(rows_all, wbuf[2].reshape(4 * HD, D))
    gated = opened * jax.nn.sigmoid(gate)
    ids = lax.broadcasted_iota(jnp.int32, (64, 4 * HD), 0)
    window = (ids // 8) % 2
    frame = t * TILE + x * 64 + (ids // 16) * 16 + core * 8 + ids % 8
    limit = jnp.where(window == 0, lens[0], lens[1])
    gated = jnp.where(frame < limit, gated, 0.0).astype(BF16)
    gx[core, 1:5] = gated.reshape(4, 16, 4 * HD)

    for cc in range(2):
        rcopy(gx.at[core, 4], gx.at[core, 0], halo_send, halo_recv, t_next, edge[cc]).start()
        rcopy(gx.at[core, 1], gx.at[core, 5], halo_send, halo_recv, t_prev, edge[cc]).start()
    inner = gx.at[core, pl.ds(1, 4)]
    rcopy(inner, inner, halo_send, halo_recv, t, sibling).start()
    bulk_wait(params.at[pl.ds(0, 3)], params_recv)
    taps = jnp.concatenate([params[k, :, 0:HD] for k in range(4)], axis=1)
    bulk_wait(gx.at[:, pl.ds(0, 4)], halo_recv)

    first = jnp.logical_and(t == 0, x == 0)
    last = jnp.logical_and(t == 15, x == 1)
    for cc in range(2):
        for j in range(6):
            block_rows = gx[cc, j].astype(F32)
            if j == 0:
                block_rows = jnp.where(first, 0.0, block_rows)
            if j == 5:
                block_rows = jnp.where(last, 0.0, block_rows)
            start = pl.multiple_of((2 * j + cc + 1 - core) * 8, 8)
            for w in range(2):
                gbuf[w, pl.ds(start, 8), :] = block_rows[w * 8 : w * 8 + 8]
    sums = [jnp.zeros((8, 4 * HD), F32) for _ in range(8)]
    for k in range(31):
        tap = taps[k : k + 1, :]
        for j in range(4):
            for w in range(2):
                row = 16 * j + 9 + k
                sums[2 * j + w] = sums[2 * j + w] + gbuf[w, row : row + 8, :] * tap
    affine = jnp.concatenate(sums, axis=0) * taps[31:32, :] + taps[32:33, :]
    activated = (affine * jax.nn.sigmoid(affine)).astype(BF16)

    weights_end(3)
    total = dot_nn(activated, wbuf[3].reshape(4 * HD, D))
    final = reduce_rows(1, total)
    out[...] = (hidden + final).reshape(2, 8, D).astype(BF16)

    bulk_wait(kv.at[pl.ds(0, 15)], kv_send)
    bulk_wait(wbuf.at[pl.ds(0, 3)], w_send)
    bulk_wait(params.at[pl.ds(0, 3)], params_send)
    bulk_wait(hsend.at[pl.ds(0, 3)], a2a_send)
    for i in range(2):
        bulk_wait(psend.at[i, pl.ds(0, 3)], p_send.at[i])
    bulk_wait(nbuf.at[pl.ds(0, 3)], n_send)
    bulk_wait(gx.at[:, pl.ds(0, 4)], halo_send)


def shards(
    features,
    lengths,
    norm_gains,
    qkv_weight,
    pos_weight,
    pos_biases,
    out_weight,
    conv_in_weight,
    depth_kernel,
    conv_scale,
    conv_shift,
    conv_out_weight,
):
    vmem = pl.BlockSpec(memory_space=pltpu.VMEM)
    hbm = pl.BlockSpec(memory_space=pl.ANY)
    dma = pltpu.SemaphoreType.DMA
    return pl.pallas_call(
        kernel,
        out_shape=jax.ShapeDtypeStruct((2, 8, D), BF16),
        in_specs=[pl.BlockSpec(memory_space=pltpu.SMEM)] + [vmem] * 3 + [hbm, vmem, hbm, hbm] + [vmem] * 3 + [hbm],
        out_specs=vmem,
        scratch_shapes=[
            pltpu.VMEM((256, D), BF16),
            pltpu.VMEM((16, 2 * HD, 256), BF16),
            pltpu.VMEM((256, HD), BF16),
            pltpu.VMEM((256, HD), BF16),
            pltpu.VMEM((TILE, HALF), F32),
            pltpu.VMEM((TILE, HALF), F32),
            pltpu.VMEM((24, HALF), F32),
            pltpu.VMEM((24, HALF), F32),
            pltpu.VMEM((17, 256, TILE), F32),
            pltpu.VMEM((16, 256, TILE), F32),
            pltpu.VMEM((4, 4, HD, D), BF16),
            pltpu.VMEM((4, 40, TILE), F32),
            pltpu.VMEM((4, 4, 16, TILE), BF16),
            pltpu.VMEM((4, 4, 16, TILE), BF16),
            pltpu.VMEM((2, 4, 16, D), BF16),
            pltpu.VMEM((2, 4, 16, D), BF16),
            pltpu.VMEM((4, 16, D), F32),
            pltpu.VMEM((4, 16, D), BF16),
            pltpu.VMEM((2, 6, 16, 4 * HD), BF16),
            pltpu.VMEM((2, 112, 4 * HD), F32),
            dma,
            dma((2, 2, 4, 2)),
            dma((2,)),
            dma,
            dma((4,)),
            dma((4,)),
            dma((4,)),
            dma,
            dma,
            dma((2,)),
            dma((2,)),
            dma,
            dma,
            dma,
            dma,
            dma,
            dma,
            pltpu.VMEM((HD, D), BF16),
            dma,
        ],
        compiler_params=pltpu.CompilerParams(
            collective_id=0, has_side_effects=True, vmem_limit_bytes=60 * 2**20
        ),
    )(
        lengths,
        features,
        norm_gains,
        qkv_weight,
        pos_weight,
        pos_biases,
        out_weight,
        conv_in_weight,
        depth_kernel,
        conv_scale.reshape(1, HD),
        conv_shift.reshape(1, HD),
        conv_out_weight,
    )


def solution(mesh):
    return jax.shard_map(
        shards,
        mesh=mesh,
        in_specs=(
            P(None, "tm", None),
            P(),
            P(),
            P(None, "tensor", None),
            P("tensor", None),
            P(None, "tensor"),
            P("tensor", None),
            P(None, "tensor", None),
            P(None, "tensor"),
            P("tensor"),
            P("tensor"),
            P("tensor", None),
        ),
        out_specs=P(None, ("tm", "tensor"), None),
        check_vma=False,
    )
```
